32 devices in a mesh: blk: 8 (over y, x, core), rep: 4 (over z).
Axes of the slice: x: 2, y: 2, z: 4, core: 2. Of those that a mesh axis runs over, the one named last changes fastest.
Arguments:
- coords: float32 [3, 1200, 2048], P(None, 'rep', 'blk'), may hold values from -40 to 40
- frame_count: int32 [8], P('blk'), may hold values from 64 to 256, as said below
Outputs:
- deviation_behind: float32 [3, 2048, 256], P(None, ('blk', 'rep'))
- deviation_ahead: float32 [3, 2048, 256], P(None, ('blk', 'rep'))
The draws below stay inside these ranges and needn't reach their ends.
Inputs may be any that keep to these rules, and one draw needn't show every extreme that they name: `frame_count`: at least one block is full and at least one holds exactly 64 frames.
All inputs are finite; a program needn't handle non-finite values.
Results may differ from the reference program's by a relative error of at most 0.0003.
Values sent between devices are 32-bit elements; how exact they have to be, the bound alone decides.
A program may use at most 64 MiB of HBM per device.

```python
import math
import jax
import jax.numpy as jnp
from jax import lax

FR_BLK = 256
NATOM = 1200
ROUNDS = 3
NEWTON = 4
BLOCKS = 8
FRAMES = 2048


def rotation_tables(quat):
    norm_q = jnp.sqrt(jnp.sum(quat * quat, axis=0))
    w_part = quat[0] / norm_q
    x_part = quat[1] / norm_q
    y_part = quat[2] / norm_q
    z_part = quat[3] / norm_q
    row_one = jnp.stack([1.0 - 2.0 * (y_part * y_part + z_part * z_part), 2.0 * (x_part * y_part - w_part * z_part), 2.0 * (x_part * z_part + w_part * y_part)], 0)
    row_two = jnp.stack([2.0 * (x_part * y_part + w_part * z_part), 1.0 - 2.0 * (x_part * x_part + z_part * z_part), 2.0 * (y_part * z_part - w_part * x_part)], 0)
    row_three = jnp.stack([2.0 * (x_part * z_part - w_part * y_part), 2.0 * (y_part * z_part + w_part * x_part), 1.0 - 2.0 * (x_part * x_part + y_part * y_part)], 0)
    return jnp.stack([row_one, row_two, row_three], 0)


def draw_coords(key, part):
    pieces = jax.random.split(key, 5)
    scales = jnp.array([1.5, 1.0, 0.6], jnp.float32).reshape(3, 1)
    structure = jax.random.normal(pieces[0], (3, NATOM), jnp.float32) * scales
    quat = jax.random.normal(pieces[4], (4, FRAMES), jnp.float32)
    rotation = rotation_tables(quat)
    rotated = jnp.einsum('klf,la->kaf', rotation, structure)
    amplitude = jnp.exp(jax.random.uniform(pieces[1], (1, 1, FRAMES), jnp.float32, math.log(0.7), math.log(2.5)))
    noise = jax.random.normal(pieces[2], (3, NATOM, FRAMES), jnp.float32)
    offset = 3.0 * jax.random.normal(pieces[3], (3, 1, FRAMES), jnp.float32)
    return jnp.clip(rotated + amplitude * noise + offset, -40.0, 40.0).astype(jnp.float32)


def draw_frame_count(key, part):
    first, second = jax.random.split(key)
    counts = jax.random.randint(first, (BLOCKS,), FR_BLK // 4, FR_BLK + 1, jnp.int32)
    chosen = jax.random.randint(second, (), 0, BLOCKS, jnp.int32)
    shortest = (chosen + 1) % BLOCKS
    indices = jnp.arange(BLOCKS, dtype=jnp.int32)
    counts = jnp.where(indices == shortest, FR_BLK // 4, counts)
    return jnp.where(indices == chosen, FR_BLK, counts).astype(jnp.int32)


def setup_inputs(seed: int = 0) -> dict:
    keys = jax.random.split(jax.random.key(seed), 3)
    coords = draw_coords(jax.random.fold_in(keys[2], 71), 0)
    frame_count = draw_frame_count(jax.random.fold_in(keys[2], 71), 0)
    return dict(coords=coords, frame_count=frame_count)


def pair_minor(upper, lower, left, right):
    return upper[left] * lower[right] - upper[right] * lower[left]


def deviation(covariance, own_sq, other_sq):
    m = [[covariance[first, :, second, :] for second in range(3)] for first in range(3)]
    keyed = [
        [m[0][0] + m[1][1] + m[2][2], m[1][2] - m[2][1], m[2][0] - m[0][2], m[0][1] - m[1][0]],
        [m[1][2] - m[2][1], m[0][0] - m[1][1] - m[2][2], m[0][1] + m[1][0], m[2][0] + m[0][2]],
        [m[2][0] - m[0][2], m[0][1] + m[1][0], -m[0][0] + m[1][1] - m[2][2], m[1][2] + m[2][1]],
        [m[0][1] - m[1][0], m[2][0] + m[0][2], m[1][2] + m[2][1], -m[0][0] - m[1][1] + m[2][2]],
    ]
    top_one, top_two, low_one, low_two = keyed
    det_key = (pair_minor(top_one, top_two, 0, 1) * pair_minor(low_one, low_two, 2, 3)
               - pair_minor(top_one, top_two, 0, 2) * pair_minor(low_one, low_two, 1, 3)
               + pair_minor(top_one, top_two, 0, 3) * pair_minor(low_one, low_two, 1, 2)
               + pair_minor(top_one, top_two, 1, 2) * pair_minor(low_one, low_two, 0, 3)
               - pair_minor(top_one, top_two, 1, 3) * pair_minor(low_one, low_two, 0, 2)
               + pair_minor(top_one, top_two, 2, 3) * pair_minor(low_one, low_two, 0, 1))
    det_three = (m[0][0] * (m[1][1] * m[2][2] - m[1][2] * m[2][1])
                 - m[0][1] * (m[1][0] * m[2][2] - m[1][2] * m[2][0])
                 + m[0][2] * (m[1][0] * m[2][1] - m[1][1] * m[2][0]))
    square_sum = m[0][0] * m[0][0]
    for first in range(3):
        for second in range(3):
            if first + second > 0:
                square_sum = square_sum + m[first][second] * m[first][second]
    second_coef = -2.0 * square_sum
    first_coef = -8.0 * det_three
    total = own_sq[:, None] + other_sq[None, :]
    largest = 0.5 * total
    for newton_step in range(NEWTON):
        squared = largest * largest
        polynomial = squared * squared + second_coef * squared + first_coef * largest + det_key
        derivative = 4.0 * squared * largest + 2.0 * second_coef * largest + first_coef
        largest = largest - polynomial / derivative
    return total - 2.0 * largest


def reference(coords, frame_count):
    centroid = jnp.sum(coords, axis=1, keepdims=True) / NATOM
    centered = coords - centroid
    self_sq = jnp.sum(centered * centered, axis=(0, 1)) / NATOM
    blocked = centered.reshape(3, NATOM, BLOCKS, FR_BLK)
    block_sq = self_sq.reshape(BLOCKS, FR_BLK)
    valid = jnp.arange(FR_BLK, dtype=jnp.int32)[None, :] < frame_count[:, None]
    behind_list = []
    ahead_list = []
    for distance in range(1, ROUNDS + 1):
        def one_pair(block, shift_by=distance):
            partner = ((block - shift_by) % BLOCKS).astype(jnp.int32)
            own_block = lax.dynamic_index_in_dim(blocked, block, 2, keepdims=False)
            partner_block = lax.dynamic_index_in_dim(blocked, partner, 2, keepdims=False)
            covariance = lax.dot_general(own_block, partner_block, (((1,), (1,)), ((), ())),
                                         precision=lax.Precision.HIGHEST) / NATOM
            own_sq = lax.dynamic_index_in_dim(block_sq, block, 0, keepdims=False)
            other_sq = lax.dynamic_index_in_dim(block_sq, partner, 0, keepdims=False)
            own_valid = lax.dynamic_index_in_dim(valid, block, 0, keepdims=False)
            other_valid = lax.dynamic_index_in_dim(valid, partner, 0, keepdims=False)
            mask = own_valid[:, None] & other_valid[None, :]
            return jnp.where(mask, deviation(covariance, own_sq, other_sq), 0.0)

        pair_blocks = lax.map(one_pair, jnp.arange(BLOCKS, dtype=jnp.int32))
        behind_list.append(pair_blocks.reshape(FRAMES, FR_BLK))
        rolled = jnp.roll(pair_blocks, -distance, axis=0)
        ahead_list.append(jnp.transpose(rolled, (0, 2, 1)).reshape(FRAMES, FR_BLK))
    return jnp.stack(behind_list, 0), jnp.stack(ahead_list, 0)
```

```python
import functools

import jax
import jax.numpy as jnp
from jax import lax
from jax.experimental import pallas as pl
from jax.experimental.pallas import tpu as pltpu
from jax.sharding import PartitionSpec as P

ROUNDS = 3
NEWTON = 4
MESH = pl.DeviceIdType.MESH


def pair_minor(upper, lower, left, right):
    return upper[left] * lower[right] - upper[right] * lower[left]


def deviation(m, total):
    keyed = [
        [m[0][0] + m[1][1] + m[2][2], m[1][2] - m[2][1], m[2][0] - m[0][2], m[0][1] - m[1][0]],
        [m[1][2] - m[2][1], m[0][0] - m[1][1] - m[2][2], m[0][1] + m[1][0], m[2][0] + m[0][2]],
        [m[2][0] - m[0][2], m[0][1] + m[1][0], -m[0][0] + m[1][1] - m[2][2], m[1][2] + m[2][1]],
        [m[0][1] - m[1][0], m[2][0] + m[0][2], m[1][2] + m[2][1], -m[0][0] - m[1][1] + m[2][2]],
    ]
    top_one, top_two, low_one, low_two = keyed
    det_key = (
        pair_minor(top_one, top_two, 0, 1) * pair_minor(low_one, low_two, 2, 3)
        - pair_minor(top_one, top_two, 0, 2) * pair_minor(low_one, low_two, 1, 3)
        + pair_minor(top_one, top_two, 0, 3) * pair_minor(low_one, low_two, 1, 2)
        + pair_minor(top_one, top_two, 1, 2) * pair_minor(low_one, low_two, 0, 3)
        - pair_minor(top_one, top_two, 1, 3) * pair_minor(low_one, low_two, 0, 2)
        + pair_minor(top_one, top_two, 2, 3) * pair_minor(low_one, low_two, 0, 1)
    )
    det_three = (
        m[0][0] * (m[1][1] * m[2][2] - m[1][2] * m[2][1])
        - m[0][1] * (m[1][0] * m[2][2] - m[1][2] * m[2][0])
        + m[0][2] * (m[1][0] * m[2][1] - m[1][1] * m[2][0])
    )
    square_sum = m[0][0] * m[0][0]
    for first in range(3):
        for second in range(3):
            if first + second > 0:
                square_sum = square_sum + m[first][second] * m[first][second]
    second_coef = -2.0 * square_sum
    first_coef = -8.0 * det_three
    largest = 0.5 * total
    for newton_step in range(NEWTON):
        squared = largest * largest
        polynomial = squared * squared + second_coef * squared + first_coef * largest + det_key
        derivative = 4.0 * squared * largest + 2.0 * second_coef * largest + first_coef
        largest = largest - polynomial / derivative
    return total - 2.0 * largest


def split(value):
    high = value.astype(jnp.bfloat16)
    low = (value - high.astype(jnp.float32)).astype(jnp.bfloat16)
    return high, low


def kernel(n, reps, coords, count, behind, ahead, own, part, cnt, pcnt, full, fth, ftl, gh, gl, cov,
           fshift, fsum, gshift, gsum, col, dev, devt,
           zs, zr, fs, xs, pr, cs, cr, os, br, ar, ls, go):
    b = lax.axis_index("blk")
    z = lax.axis_index("rep")
    par = lax.rem(b, 2)
    odd = lax.rem(b // 2, 2)
    bent = odd * par == 1
    bends = odd * (1 - par) == 1
    atoms = coords.shape[1]
    half = coords.shape[2] // 2
    quarter = half // 2
    natom = atoms * reps
    g = z // 2
    o = 1 - g
    me = z
    fd = (reps - 1) * g
    of = reps - 1 - fd
    ot = reps - 1 - z
    wk = 1 + g
    inner = jnp.minimum(z, 1) * jnp.minimum(reps - 1 - z, 1)

    def at(step):
        return lax.rem(b + step + n, n)

    barrier = pltpu.get_barrier_semaphore()
    for step in (1 - 2 * par, 2 - 4 * odd, 6 * par - 3):
        pl.semaphore_signal(barrier, inc=1, device_id=(at(step), z), device_id_type=MESH)

    @pl.when(odd + par == 1)
    def _():
        pl.semaphore_signal(barrier, inc=1, device_id=(at(1 - 2 * odd), z), device_id_type=MESH)

    @pl.when(z > 0)
    def _():
        pl.semaphore_signal(barrier, inc=1, device_id=(b, z - 1), device_id_type=MESH)

    @pl.when(z < reps - 1)
    def _():
        pl.semaphore_signal(barrier, inc=1, device_id=(b, z + 1), device_id_type=MESH)

    pl.semaphore_wait(barrier, 4 + lax.rem(odd + par, 2) + inner)

    @pl.when((odd == 0) & (par == 1))
    def _():
        pl.semaphore_signal(go, inc=1, device_id=(at(1), z), device_id_type=MESH)

    def remote(src, dst, send, recv, where):
        return pltpu.make_async_remote_copy(src_ref=src, dst_ref=dst, send_sem=send, recv_sem=recv,
                                            device_id=where, device_id_type=MESH)

    def lanes(h):
        return pl.ds(pl.multiple_of(h * half, half), half)

    def source(s, h, k, mine):
        return coords.at[k, :, lanes(h)] if mine else own.at[s, h, k]

    def along(s, h, k, mine, where):
        return remote(source(s, h, k, mine), own.at[s, h, k], zs.at[1 - mine, h, k], zr.at[s, h, k],
                      (b, where))

    def first(s, k, mine):
        slot = 2 * par
        return remote(source(s, g, k, mine), part.at[slot, s, k], xs.at[1, s, k], pr.at[slot, s, k],
                      (at(1 + slot), z))

    def second(s, k, mine):
        return remote(source(s, g, k, mine), part.at[1, s, k], xs.at[0, s, k], pr.at[1, s, k],
                      (at(2), z))

    def bend(s, k):
        return remote(part.at[2, s, k], part.at[1, s, k], xs.at[3, s, k], pr.at[1, s, k],
                      (at(-1), z))

    def relay(s, k):
        slot = 2 - 2 * par
        return remote(part.at[1, s, k], part.at[slot, s, k], xs.at[2, s, k], pr.at[slot, s, k],
                      (at(1 - 2 * par), z))

    def feed(slot, k):
        return remote(part.at[slot, z, k], part.at[slot, z, k], fs.at[slot, k], pr.at[slot, z, k],
                      (b, wk))

    def count_first():
        slot = 2 * par
        return remote(cnt, pcnt.at[slot], cs.at[1], cr.at[slot], (at(1 + slot), z))

    def count_second():
        return remote(cnt, pcnt.at[1], cs.at[0], cr.at[1], (at(2), z))

    def count_bend():
        return remote(pcnt.at[2], pcnt.at[1], cs.at[3], cr.at[1], (at(-1), z))

    def count_relay():
        slot = 2 - 2 * par
        return remote(pcnt.at[1], pcnt.at[slot], cs.at[2], cr.at[slot], (at(1 - 2 * par), z))

    def zr_wait(s, h, k):
        remote(own.at[s, h, k], own.at[s, h, k], zs.at[0, h, k], zr.at[s, h, k],
               (b, lax.rem(z + 1, reps))).wait_recv()

    def pr_wait(d, s, k):
        remote(part.at[d, s, k], part.at[d, s, k], xs.at[0, s, k], pr.at[d, s, k],
               (b, lax.rem(z + 1, reps))).wait_recv()

    def cr_wait(d):
        remote(pcnt.at[d], pcnt.at[d], cs.at[0], cr.at[d], (b, lax.rem(z + 1, reps))).wait_recv()

    def local(h):
        return pltpu.make_async_copy(coords.at[:, :, lanes(h)], own.at[z, h], ls.at[h])

    def behind_copy(h, d, j):
        return remote(dev.at[h, d, pl.ds(j * quarter, quarter)], behind.at[d, :, lanes(g)],
                      os.at[h, d, 2 + j], br.at[d, g], (b, 2 * h + j))

    def ahead_copy(h, d, j):
        return remote(devt.at[h, d, pl.ds(j * quarter, quarter)], ahead.at[d, :, lanes(h)],
                      os.at[h, d, j], ar.at[d, h], (lax.rem(b - 1 - d + n, n), 2 * g + j))

    def ahead_wait(d, h):
        remote(devt.at[0, d, pl.ds(0, quarter)], ahead.at[d, :, pl.ds(h * half, half)],
               os.at[0, d, 0], ar.at[d, h], (at(1), z)).wait_recv()

    def behind_wait(d, side):
        remote(dev.at[0, d, pl.ds(0, quarter)], behind.at[d, :, lanes(side)],
               os.at[0, d, 2], br.at[d, side], (at(1), z)).wait_recv()

    def feeder():
        for k in range(3):
            along(me, o, k, True, wk).start()

            @pl.when(par == 1)
            def _(k=k):
                first(me, k, True).start()

        @pl.when(bends)
        def _():
            pl.semaphore_wait(go, 1)

        for k in range(3):
            @pl.when(jnp.logical_not(bent))
            def _(k=k):
                second(me, k, True).start()

        for k in range(3):
            along(me, g, k, True, wk).start()
        for k in range(3):
            @pl.when(par == 0)
            def _(k=k):
                pr_wait(2, me, k)

                @pl.when(bends)
                def _():
                    bend(me, k).start()

                feed(2, k).start()

        for k in range(3):
            pr_wait(1, me, k)
            feed(1, k).start()
        for k in range(3):
            along(me, o, k, True, wk).wait_send()
            along(me, g, k, True, wk).wait_send()
            feed(1, k).wait_send()

            @pl.when(par == 0)
            def _(k=k):
                feed(2, k).wait_send()

            @pl.when(par == 1)
            def _(k=k):
                first(me, k, True).wait_send()

            @pl.when(jnp.logical_not(bent))
            def _(k=k):
                second(me, k, True).wait_send()

            @pl.when(bends)
            def _(k=k):
                bend(me, k).wait_send()

        for d in range(ROUNDS):
            for side in range(2):
                behind_wait(d, side)
                ahead_wait(d, side)

    def across(s, k, mine):
        first(s, k, mine).start()

        @pl.when(jnp.logical_not(bent))
        def _():
            second(s, k, mine).start()

    def turn(s, k):
        @pl.when(bends)
        def _():
            pr_wait(2, s, k)
            bend(s, k).start()

    def pass_on(s, k):
        pr_wait(1, s, k)
        relay(s, k).start()

    def settle(s, bent_in):
        for k in range(3):
            pr_wait(0, s, k)

            if bent_in:
                @pl.when(jnp.logical_not(bends))
                def _(k=k):
                    pr_wait(2, s, k)
            else:
                pr_wait(2, s, k)

    def own_part(s, h, k, start):
        value = own[s, h, k]
        if start:
            shift = jnp.sum(value, axis=0, keepdims=True) / atoms
            fshift[h, k, 0:1, :] = shift
        else:
            shift = fshift[h, k, 0:1, :]
        value = value - shift
        full[0:atoms, :] = value
        total = jnp.sum(value, axis=0, keepdims=True)
        square = jnp.sum(value * value, axis=0, keepdims=True)
        fsum[h, k, 0:1, :] = fsum[h, k, 0:1, :] + total
        fsum[h, 3, 0:1, :] = fsum[h, 3, 0:1, :] + square
        high, low = split(full[...].T)
        fth[h, s, k * half:(k + 1) * half, :] = high
        ftl[h, s, k * half:(k + 1) * half, :] = low

    def partner_part(s, start):
        def one(d, carry):
            for k in range(3):
                value = part[d, s, k]
                if start:
                    shift = jnp.sum(value, axis=0, keepdims=True) / atoms
                    gshift[d, k, 0:1, :] = shift
                else:
                    shift = gshift[d, k, 0:1, :]
                value = value - shift
                total = jnp.sum(value, axis=0, keepdims=True)
                square = jnp.sum(value * value, axis=0, keepdims=True)
                gsum[d, k, 0:1, :] = gsum[d, k, 0:1, :] + total
                gsum[d, 3, 0:1, :] = gsum[d, 3, 0:1, :] + square
                high, low = split(value)
                gh[d, s, 0:atoms, k * half:(k + 1) * half] = high
                gl[d, s, 0:atoms, k * half:(k + 1) * half] = low
            return carry

        lax.fori_loop(0, ROUNDS, one, 0)

    product = functools.partial(jnp.dot, preferred_element_type=jnp.float32)

    def multiply(s, h):
        def one(d, carry):
            cov[h, d] = cov[h, d] + (product(fth[h, s], gh[d, s]) + product(fth[h, s], gl[d, s])
                                     + product(ftl[h, s], gh[d, s]))
            return carry

        lax.fori_loop(0, ROUNDS, one, 0)

    def multiply_rows(s, h, k):
        rows = slice(k * half, (k + 1) * half)

        def one(d, carry):
            high, low = fth[h, s, rows, :], ftl[h, s, rows, :]
            cov[h, d, rows, :] = cov[h, d, rows, :] + (
                product(high, gh[d, s]) + product(high, gl[d, s]) + product(low, gh[d, s]))
            return carry

        lax.fori_loop(0, ROUNDS, one, 0)

    def tile(h):
        square = fsum[h, 3, 0:1, :] / natom
        for k in range(3):
            mean = fsum[h, k, 0:1, :] / natom
            square = square - mean * mean
            col[k] = jnp.broadcast_to(mean, (half, half)).T
        col[3] = jnp.broadcast_to(square, (half, half)).T
        rows = half // 4

        def block(d, carry):
            mean = [gsum[d, k, 0:1, :] / natom for k in range(3)]
            other_square = gsum[d, 3, 0:1, :] / natom
            for k in range(3):
                other_square = other_square - mean[k] * mean[k]

            def chunk(i, inner_carry):
                r = pl.multiple_of(i * rows, rows)
                m = [[cov[h, d, pl.ds(k * half + r, rows), l * half:(l + 1) * half] * (1.0 / natom)
                      - col[k, pl.ds(r, rows), :] * mean[l] for l in range(3)] for k in range(3)]
                total = col[3, pl.ds(r, rows), :] + other_square
                frame = h * half + r + lax.broadcasted_iota(jnp.int32, (rows, half), 0)
                other = g * half + lax.broadcasted_iota(jnp.int32, (rows, half), 1)
                mask = (frame < cnt[0:1, :]) & (other < pcnt[d, 0:1, :])
                dev[h, d, pl.ds(r, rows), :] = jnp.where(mask, deviation(m, total), 0.0)
                return inner_carry

            lax.fori_loop(0, half // rows, chunk, 0)
            devt[h, d] = dev[h, d].T
            for j in range(2):
                @pl.when(2 * h + j != z)
                def _(j=j):
                    behind_copy(h, d, j).start()

                @pl.when(2 * h + j == z)
                def _(j=j):
                    behind[d, :, lanes(g)] = dev[h, d, j * quarter:(j + 1) * quarter, :]

                ahead_copy(h, d, j).start()
            return carry

        lax.fori_loop(0, ROUNDS, block, 0)

    def worker():
        for k in range(3):
            along(me, o, k, True, ot).start()
            first(me, k, True).start()

        @pl.when(bends)
        def _():
            pl.semaphore_wait(go, 1)

        for k in range(3):
            @pl.when(jnp.logical_not(bent))
            def _(k=k):
                second(me, k, True).start()

        along(me, g, 0, True, ot).start()
        for h in range(2):
            local(h).start()
        cnt[...] = jnp.full(cnt.shape, count[0], jnp.int32)
        count_first().start()

        @pl.when(jnp.logical_not(bent))
        def _():
            count_second().start()

        full[...] = jnp.zeros_like(full)
        fsum[...] = jnp.zeros_like(fsum)
        gsum[...] = jnp.zeros_like(gsum)
        for k in range(3):
            zr_wait(fd, o, k)
            along(fd, o, k, False, ot).start()
            zr_wait(ot, g, k)
            across(ot, k, False)
            turn(me, k)

        @pl.when(bends)
        def _():
            cr_wait(2)
            count_bend().start()

        for k in range(1, 3):
            along(me, g, k, True, ot).start()
        for k in range(3):
            pass_on(me, k)
        cr_wait(1)
        count_relay().start()
        cov[...] = jnp.zeros_like(cov)
        gh[...] = jnp.zeros_like(gh)
        gl[...] = jnp.zeros_like(gl)
        for h in range(2):
            local(h).wait()
        for h in range(2):
            for k in range(3):
                own_part(me, h, k, True)
        for k in range(3):
            zr_wait(fd, g, k)
            along(fd, g, k, False, ot).start()

            @pl.when(par == 0)
            def _(k=k):
                first(fd, k, False).start()

            zr_wait(of, g, k)
            across(of, k, False)
            turn(ot, k)

        settle(me, True)
        partner_part(me, True)
        for h in range(2):
            multiply(me, h)
        for k in range(3):
            turn(of, k)
        for k in range(3):
            pass_on(ot, k)
        for k in range(3):
            own_part(ot, g, k, False)
        settle(ot, True)
        partner_part(ot, False)
        multiply(ot, g)
        for h in range(2):
            for k in range(3):
                own_part(fd, h, k, False)
        for k in range(3):
            own_part(of, g, k, False)
        for k in range(3):
            pass_on(of, k)
        for k in range(3):
            zr_wait(ot, o, k)
            own_part(ot, o, k, False)
        multiply(ot, o)
        settle(of, True)
        partner_part(of, False)
        multiply(of, g)
        for k in range(3):
            pass_on(fd, k)
        for k in range(3):
            pr_wait(0, fd, k)
            pr_wait(2, fd, k)
        partner_part(fd, False)
        for h in range(2):
            multiply(fd, h)
        cr_wait(0)

        @pl.when(jnp.logical_not(bends))
        def _():
            cr_wait(2)

        tile(g)
        for k in range(3):
            zr_wait(of, o, k)
            own_part(of, o, k, False)
            multiply_rows(of, o, k)
        tile(o)
        finish()

    def finish():
        for k in range(3):
            for h in range(2):
                along(me, h, k, True, ot).wait_send()
                along(fd, h, k, False, ot).wait_send()
            for s in (me, ot, of):
                first(s, k, False).wait_send()
                relay(s, k).wait_send()

                @pl.when(jnp.logical_not(bent))
                def _(s=s, k=k):
                    second(s, k, False).wait_send()

                @pl.when(bends)
                def _(s=s, k=k):
                    bend(s, k).wait_send()

            relay(fd, k).wait_send()

            @pl.when(par == 0)
            def _(k=k):
                first(fd, k, False).wait_send()

        count_first().wait_send()
        count_relay().wait_send()

        @pl.when(jnp.logical_not(bent))
        def _():
            count_second().wait_send()

        @pl.when(bends)
        def _():
            count_bend().wait_send()

        for d in range(ROUNDS):
            for h in range(2):
                for j in range(2):
                    ahead_copy(h, d, j).wait_send()

                    @pl.when(2 * h + j != z)
                    def _(h=h, d=d, j=j):
                        behind_copy(h, d, j).wait_send()

                ahead_wait(d, h)
            behind_wait(d, o)

    @pl.when(inner == 0)
    def _():
        feeder()

    @pl.when(inner == 1)
    def _():
        worker()


def shards(n, reps, coords, frame_count):
    atoms, frames = coords.shape[1], coords.shape[2]
    half = frames // 2
    depth = (atoms + 127) // 128 * 128
    f32, bf16 = jnp.float32, jnp.bfloat16
    dma = pltpu.SemaphoreType.DMA
    vmem = pl.BlockSpec(memory_space=pltpu.VMEM)
    result = jax.ShapeDtypeStruct((ROUNDS, frames // reps, frames), f32)
    return pl.pallas_call(
        functools.partial(kernel, n, reps),
        out_shape=(result, result),
        in_specs=[pl.BlockSpec(memory_space=pl.ANY), pl.BlockSpec(memory_space=pltpu.SMEM)],
        out_specs=(vmem, vmem),
        scratch_shapes=[
            pltpu.VMEM((reps, 2, 3, atoms, half), f32),
            pltpu.VMEM((ROUNDS, reps, 3, atoms, half), f32),
            pltpu.VMEM((8, half), jnp.int32),
            pltpu.VMEM((ROUNDS, 8, half), jnp.int32),
            pltpu.VMEM((depth, half), f32),
            pltpu.VMEM((2, reps, 3 * half, depth), bf16),
            pltpu.VMEM((2, reps, 3 * half, depth), bf16),
            pltpu.VMEM((ROUNDS, reps, depth, 3 * half), bf16),
            pltpu.VMEM((ROUNDS, reps, depth, 3 * half), bf16),
            pltpu.VMEM((2, ROUNDS, 3 * half, 3 * half), f32),
            pltpu.VMEM((2, 3, 8, half), f32),
            pltpu.VMEM((2, 4, 8, half), f32),
            pltpu.VMEM((ROUNDS, 3, 8, half), f32),
            pltpu.VMEM((ROUNDS, 4, 8, half), f32),
            pltpu.VMEM((4, half, half), f32),
            pltpu.VMEM((2, ROUNDS, half, half), f32),
            pltpu.VMEM((2, ROUNDS, half, half), f32),
            dma((2, 2, 3)),
            dma((reps, 2, 3)),
            dma((ROUNDS, 3)),
            dma((4, reps, 3)),
            dma((ROUNDS, reps, 3)),
            dma((4,)),
            dma((ROUNDS,)),
            dma((2, ROUNDS, 4)),
            dma((ROUNDS, 2)),
            dma((ROUNDS, 2)),
            dma((2,)),
            pltpu.SemaphoreType.REGULAR,
        ],
        compiler_params=pltpu.CompilerParams(collective_id=0, has_side_effects=True,
                                             vmem_limit_bytes=48 * 1024 * 1024),
    )(coords, frame_count.astype(jnp.int32))


def solution(mesh):
    in_specs = (P(None, "rep", "blk"), P("blk"))
    out_specs = (P(None, ("blk", "rep"), None), P(None, ("blk", "rep"), None))
    body = functools.partial(shards, mesh.shape["blk"], mesh.shape["rep"])
    return jax.shard_map(body, mesh=mesh, in_specs=in_specs, out_specs=out_specs, check_vma=False)
```

```python
import functools

import jax
import jax.numpy as jnp
from jax import lax
from jax.experimental import pallas as pl
from jax.experimental.pallas import tpu as pltpu
from jax.sharding import PartitionSpec as P

ROUNDS = 3
NEWTON = 4
MESH = pl.DeviceIdType.MESH


def pair_minor(upper, lower, left, right):
    return upper[left] * lower[right] - upper[right] * lower[left]


def deviation(m, total):
    keyed = [
        [m[0][0] + m[1][1] + m[2][2], m[1][2] - m[2][1], m[2][0] - m[0][2], m[0][1] - m[1][0]],
        [m[1][2] - m[2][1], m[0][0] - m[1][1] - m[2][2], m[0][1] + m[1][0], m[2][0] + m[0][2]],
        [m[2][0] - m[0][2], m[0][1] + m[1][0], -m[0][0] + m[1][1] - m[2][2], m[1][2] + m[2][1]],
        [m[0][1] - m[1][0], m[2][0] + m[0][2], m[1][2] + m[2][1], -m[0][0] - m[1][1] + m[2][2]],
    ]
    top_one, top_two, low_one, low_two = keyed
    det_key = (
        pair_minor(top_one, top_two, 0, 1) * pair_minor(low_one, low_two, 2, 3)
        - pair_minor(top_one, top_two, 0, 2) * pair_minor(low_one, low_two, 1, 3)
        + pair_minor(top_one, top_two, 0, 3) * pair_minor(low_one, low_two, 1, 2)
        + pair_minor(top_one, top_two, 1, 2) * pair_minor(low_one, low_two, 0, 3)
        - pair_minor(top_one, top_two, 1, 3) * pair_minor(low_one, low_two, 0, 2)
        + pair_minor(top_one, top_two, 2, 3) * pair_minor(low_one, low_two, 0, 1)
    )
    det_three = (
        m[0][0] * (m[1][1] * m[2][2] - m[1][2] * m[2][1])
        - m[0][1] * (m[1][0] * m[2][2] - m[1][2] * m[2][0])
        + m[0][2] * (m[1][0] * m[2][1] - m[1][1] * m[2][0])
    )
    square_sum = m[0][0] * m[0][0]
    for first in range(3):
        for second in range(3):
            if first + second > 0:
                square_sum = square_sum + m[first][second] * m[first][second]
    second_coef = -2.0 * square_sum
    first_coef = -8.0 * det_three
    largest = 0.5 * total
    for newton_step in range(NEWTON):
        squared = largest * largest
        polynomial = squared * squared + second_coef * squared + first_coef * largest + det_key
        derivative = 4.0 * squared * largest + 2.0 * second_coef * largest + first_coef
        largest = largest - polynomial / derivative
    return total - 2.0 * largest


def split(value):
    high = value.astype(jnp.bfloat16)
    low = (value - high.astype(jnp.float32)).astype(jnp.bfloat16)
    return high, low


def kernel(n, reps, coords, count, behind, ahead, own, part, cnt, pcnt, full, ft, gt, cov,
           fshift, fsum, gshift, gsum, col, dev, devt,
           zs, zr, fs, xs, pr, cs, cr, os, br, ar, ls, go):
    b = lax.axis_index("blk")
    z = lax.axis_index("rep")
    par = lax.rem(b, 2)
    odd = lax.rem(b // 2, 2)
    bent = odd * par == 1
    bends = odd * (1 - par) == 1
    atoms = coords.shape[1]
    half = coords.shape[2] // 2
    quarter = half // 2
    natom = atoms * reps
    pitch = (atoms + 15) // 16 * 16
    again = full.shape[0]
    tail = ft.shape[3] - again
    g = z // 2
    o = 1 - g
    me = z
    fd = (reps - 1) * g
    of = reps - 1 - fd
    ot = reps - 1 - z
    wk = 1 + g
    inner = jnp.minimum(z, 1) * jnp.minimum(reps - 1 - z, 1)

    def at(step):
        return lax.rem(b + step + n, n)

    barrier = pltpu.get_barrier_semaphore()
    for step in (1 - 2 * par, 2 - 4 * odd, 6 * par - 3):
        pl.semaphore_signal(barrier, inc=1, device_id=(at(step), z), device_id_type=MESH)

    @pl.when(odd + par == 1)
    def _():
        pl.semaphore_signal(barrier, inc=1, device_id=(at(1 - 2 * odd), z), device_id_type=MESH)

    @pl.when(z > 0)
    def _():
        pl.semaphore_signal(barrier, inc=1, device_id=(b, z - 1), device_id_type=MESH)

    @pl.when(z < reps - 1)
    def _():
        pl.semaphore_signal(barrier, inc=1, device_id=(b, z + 1), device_id_type=MESH)

    pl.semaphore_wait(barrier, 4 + lax.rem(odd + par, 2) + inner)

    @pl.when((odd == 0) & (par == 1))
    def _():
        pl.semaphore_signal(go, inc=1, device_id=(at(1), z), device_id_type=MESH)

    def remote(src, dst, send, recv, where):
        return pltpu.make_async_remote_copy(src_ref=src, dst_ref=dst, send_sem=send, recv_sem=recv,
                                            device_id=where, device_id_type=MESH)

    def lanes(h):
        return pl.ds(pl.multiple_of(h * half, half), half)

    def source(s, h, k, mine):
        return coords.at[k, :, lanes(h)] if mine else own.at[s, h, k]

    def along(s, h, k, mine, where):
        return remote(source(s, h, k, mine), own.at[s, h, k], zs.at[1 - mine, h, k], zr.at[s, h, k],
                      (b, where))

    def first(s, k, mine):
        slot = 2 * par
        return remote(source(s, g, k, mine), part.at[slot, s, k], xs.at[1, s, k], pr.at[slot, s, k],
                      (at(1 + slot), z))

    def second(s, k, mine):
        return remote(source(s, g, k, mine), part.at[1, s, k], xs.at[0, s, k], pr.at[1, s, k],
                      (at(2), z))

    def bend(s, k):
        return remote(part.at[2, s, k], part.at[1, s, k], xs.at[3, s, k], pr.at[1, s, k],
                      (at(-1), z))

    def relay(s, k):
        slot = 2 - 2 * par
        return remote(part.at[1, s, k], part.at[slot, s, k], xs.at[2, s, k], pr.at[slot, s, k],
                      (at(1 - 2 * par), z))

    def feed(slot, k):
        return remote(part.at[slot, z, k], part.at[slot, z, k], fs.at[slot, k], pr.at[slot, z, k],
                      (b, wk))

    def count_first():
        slot = 2 * par
        return remote(cnt, pcnt.at[slot], cs.at[1], cr.at[slot], (at(1 + slot), z))

    def count_second():
        return remote(cnt, pcnt.at[1], cs.at[0], cr.at[1], (at(2), z))

    def count_bend():
        return remote(pcnt.at[2], pcnt.at[1], cs.at[3], cr.at[1], (at(-1), z))

    def count_relay():
        slot = 2 - 2 * par
        return remote(pcnt.at[1], pcnt.at[slot], cs.at[2], cr.at[slot], (at(1 - 2 * par), z))

    def zr_wait(s, h, k):
        remote(own.at[s, h, k], own.at[s, h, k], zs.at[0, h, k], zr.at[s, h, k],
               (b, lax.rem(z + 1, reps))).wait_recv()

    def pr_wait(d, s, k):
        remote(part.at[d, s, k], part.at[d, s, k], xs.at[0, s, k], pr.at[d, s, k],
               (b, lax.rem(z + 1, reps))).wait_recv()

    def cr_wait(d):
        remote(pcnt.at[d], pcnt.at[d], cs.at[0], cr.at[d], (b, lax.rem(z + 1, reps))).wait_recv()

    def local(h):
        return pltpu.make_async_copy(coords.at[:, :, lanes(h)], own.at[z, h], ls.at[h])

    def behind_copy(h, d, j):
        return remote(dev.at[h, d, pl.ds(j * quarter, quarter)], behind.at[d, :, lanes(g)],
                      os.at[h, d, 2 + j], br.at[d, g], (b, 2 * h + j))

    def ahead_copy(h, d, j):
        return remote(devt.at[h, d, pl.ds(j * quarter, quarter)], ahead.at[d, :, lanes(h)],
                      os.at[h, d, j], ar.at[d, h], (lax.rem(b - 1 - d + n, n), 2 * g + j))

    def ahead_wait(d, h):
        remote(devt.at[0, d, pl.ds(0, quarter)], ahead.at[d, :, pl.ds(h * half, half)],
               os.at[0, d, 0], ar.at[d, h], (at(1), z)).wait_recv()

    def behind_wait(d, side):
        remote(dev.at[0, d, pl.ds(0, quarter)], behind.at[d, :, lanes(side)],
               os.at[0, d, 2], br.at[d, side], (at(1), z)).wait_recv()

    def feeder():
        for k in range(3):
            along(me, o, k, True, wk).start()

            @pl.when(par == 1)
            def _(k=k):
                first(me, k, True).start()

        @pl.when(bends)
        def _():
            pl.semaphore_wait(go, 1)

        for k in range(3):
            @pl.when(jnp.logical_not(bent))
            def _(k=k):
                second(me, k, True).start()

        for k in range(3):
            along(me, g, k, True, wk).start()
        for k in range(3):
            @pl.when(par == 0)
            def _(k=k):
                pr_wait(2, me, k)

                @pl.when(bends)
                def _():
                    bend(me, k).start()

                feed(2, k).start()

        for k in range(3):
            pr_wait(1, me, k)
            feed(1, k).start()
        for k in range(3):
            along(me, o, k, True, wk).wait_send()
            along(me, g, k, True, wk).wait_send()
            feed(1, k).wait_send()

            @pl.when(par == 0)
            def _(k=k):
                feed(2, k).wait_send()

            @pl.when(par == 1)
            def _(k=k):
                first(me, k, True).wait_send()

            @pl.when(jnp.logical_not(bent))
            def _(k=k):
                second(me, k, True).wait_send()

            @pl.when(bends)
            def _(k=k):
                bend(me, k).wait_send()

        for d in range(ROUNDS):
            for side in range(2):
                behind_wait(d, side)
                ahead_wait(d, side)

    def across(s, k, mine):
        first(s, k, mine).start()

        @pl.when(jnp.logical_not(bent))
        def _():
            second(s, k, mine).start()

    def turn(s, k):
        @pl.when(bends)
        def _():
            pr_wait(2, s, k)
            bend(s, k).start()

    def pass_on(s, k):
        pr_wait(1, s, k)
        relay(s, k).start()

    def settle(s, bent_in):
        for k in range(3):
            pr_wait(0, s, k)

            if bent_in:
                @pl.when(jnp.logical_not(bends))
                def _(k=k):
                    pr_wait(2, s, k)
            else:
                pr_wait(2, s, k)

    def own_part(s, h, k, start):
        value = own[s, h, k]
        if start:
            shift = jnp.sum(value, axis=0, keepdims=True) / atoms
            fshift[h, k, 0:1, :] = shift
        else:
            shift = fshift[h, k, 0:1, :]
        value = value - shift
        total = jnp.sum(value, axis=0, keepdims=True)
        square = jnp.sum(value * value, axis=0, keepdims=True)
        fsum[h, k, 0:1, :] = fsum[h, k, 0:1, :] + total
        fsum[h, 3, 0:1, :] = fsum[h, 3, 0:1, :] + square
        high = value.astype(jnp.bfloat16).astype(jnp.float32)
        full[0:atoms, :] = high
        full[pitch:pitch + atoms, :] = value - high
        turned = full[...].T.astype(jnp.bfloat16)
        ft[h, s, k * half:(k + 1) * half, 0:again] = turned
        ft[h, s, k * half:(k + 1) * half, again:again + tail] = turned[:, 0:tail]

    def partner_part(s, start):
        for d in range(ROUNDS):
            for k in range(3):
                value = part[d, s, k]
                if start:
                    shift = jnp.sum(value, axis=0, keepdims=True) / atoms
                    gshift[d, k, 0:1, :] = shift
                else:
                    shift = gshift[d, k, 0:1, :]
                value = value - shift
                total = jnp.sum(value, axis=0, keepdims=True)
                square = jnp.sum(value * value, axis=0, keepdims=True)
                gsum[d, k, 0:1, :] = gsum[d, k, 0:1, :] + total
                gsum[d, 3, 0:1, :] = gsum[d, 3, 0:1, :] + square
                high, low = split(value)
                place = slice((3 * d + k) * half, (3 * d + k + 1) * half)
                gt[s, 0:atoms, place] = high
                gt[s, pitch:pitch + atoms, place] = high
                gt[s, again:again + atoms, place] = low

    product = functools.partial(jnp.dot, preferred_element_type=jnp.float32)

    def multiply(s, h, start=False):
        term = product(ft[h, s], gt[s])
        cov[h] = term if start else cov[h] + term

    def multiply_rows(s, h, k):
        rows = slice(k * half, (k + 1) * half)
        cov[h, rows, :] = cov[h, rows, :] + product(ft[h, s, rows, :], gt[s])

    def tile(h):
        square = fsum[h, 3, 0:1, :] / natom
        for k in range(3):
            mean = fsum[h, k, 0:1, :] / natom
            square = square - mean * mean
            col[k] = jnp.broadcast_to(mean, (half, half)).T
        col[3] = jnp.broadcast_to(square, (half, half)).T
        rows = half // 4

        def block(d, carry):
            mean = [gsum[d, k, 0:1, :] / natom for k in range(3)]
            other_square = gsum[d, 3, 0:1, :] / natom
            for k in range(3):
                other_square = other_square - mean[k] * mean[k]

            def chunk(i, inner_carry):
                r = pl.multiple_of(i * rows, rows)
                m = [[cov[h, pl.ds(k * half + r, rows), lanes(3 * d + l)] * (1.0 / natom)
                      - col[k, pl.ds(r, rows), :] * mean[l] for l in range(3)] for k in range(3)]
                total = col[3, pl.ds(r, rows), :] + other_square
                frame = h * half + r + lax.broadcasted_iota(jnp.int32, (rows, half), 0)
                other = g * half + lax.broadcasted_iota(jnp.int32, (rows, half), 1)
                mask = (frame < cnt[0:1, :]) & (other < pcnt[d, 0:1, :])
                dev[h, d, pl.ds(r, rows), :] = jnp.where(mask, deviation(m, total), 0.0)
                return inner_carry

            lax.fori_loop(0, half // rows, chunk, 0)
            devt[h, d] = dev[h, d].T
            for j in range(2):
                @pl.when(2 * h + j != z)
                def _(j=j):
                    behind_copy(h, d, j).start()

                @pl.when(2 * h + j == z)
                def _(j=j):
                    behind[d, :, lanes(g)] = dev[h, d, j * quarter:(j + 1) * quarter, :]

                ahead_copy(h, d, j).start()
            return carry

        lax.fori_loop(0, ROUNDS, block, 0)

    def worker():
        for k in range(3):
            along(me, o, k, True, ot).start()
            first(me, k, True).start()

        @pl.when(bends)
        def _():
            pl.semaphore_wait(go, 1)

        for k in range(3):
            @pl.when(jnp.logical_not(bent))
            def _(k=k):
                second(me, k, True).start()

        along(me, g, 0, True, ot).start()
        for h in range(2):
            local(h).start()
        cnt[...] = jnp.full(cnt.shape, count[0], jnp.int32)
        count_first().start()

        @pl.when(jnp.logical_not(bent))
        def _():
            count_second().start()

        full[...] = jnp.zeros_like(full)
        fsum[...] = jnp.zeros_like(fsum)
        gsum[...] = jnp.zeros_like(gsum)
        for k in range(3):
            zr_wait(fd, o, k)
            along(fd, o, k, False, ot).start()
            zr_wait(ot, g, k)
            across(ot, k, False)
            turn(me, k)

        @pl.when(bends)
        def _():
            cr_wait(2)
            count_bend().start()

        for k in range(1, 3):
            along(me, g, k, True, ot).start()
        for k in range(3):
            pass_on(me, k)
        cr_wait(1)
        count_relay().start()
        gt[...] = jnp.zeros_like(gt)
        for h in range(2):
            local(h).wait()
        for h in range(2):
            for k in range(3):
                own_part(me, h, k, True)
        for k in range(3):
            zr_wait(fd, g, k)
            along(fd, g, k, False, ot).start()

            @pl.when(par == 0)
            def _(k=k):
                first(fd, k, False).start()

            zr_wait(of, g, k)
            across(of, k, False)
            turn(ot, k)

        settle(me, True)
        partner_part(me, True)
        for h in range(2):
            multiply(me, h, True)
        for k in range(3):
            turn(of, k)
        for k in range(3):
            pass_on(ot, k)
        for k in range(3):
            own_part(ot, g, k, False)
        settle(ot, True)
        partner_part(ot, False)
        multiply(ot, g)
        for h in range(2):
            for k in range(3):
                own_part(fd, h, k, False)
        for k in range(3):
            own_part(of, g, k, False)
        for k in range(3):
            pass_on(of, k)
        for k in range(3):
            zr_wait(ot, o, k)
            own_part(ot, o, k, False)
        multiply(ot, o)
        settle(of, True)
        partner_part(of, False)
        multiply(of, g)
        for k in range(3):
            pass_on(fd, k)
        for k in range(3):
            pr_wait(0, fd, k)
            pr_wait(2, fd, k)
        partner_part(fd, False)
        for h in range(2):
            multiply(fd, h)
        cr_wait(0)

        @pl.when(jnp.logical_not(bends))
        def _():
            cr_wait(2)

        tile(g)
        for k in range(3):
            zr_wait(of, o, k)
            own_part(of, o, k, False)
            multiply_rows(of, o, k)
        tile(o)
        finish()

    def finish():
        for k in range(3):
            for h in range(2):
                along(me, h, k, True, ot).wait_send()
                along(fd, h, k, False, ot).wait_send()
            for s in (me, ot, of):
                first(s, k, False).wait_send()
                relay(s, k).wait_send()

                @pl.when(jnp.logical_not(bent))
                def _(s=s, k=k):
                    second(s, k, False).wait_send()

                @pl.when(bends)
                def _(s=s, k=k):
                    bend(s, k).wait_send()

            relay(fd, k).wait_send()

            @pl.when(par == 0)
            def _(k=k):
                first(fd, k, False).wait_send()

        count_first().wait_send()
        count_relay().wait_send()

        @pl.when(jnp.logical_not(bent))
        def _():
            count_second().wait_send()

        @pl.when(bends)
        def _():
            count_bend().wait_send()

        for d in range(ROUNDS):
            for h in range(2):
                for j in range(2):
                    ahead_copy(h, d, j).wait_send()

                    @pl.when(2 * h + j != z)
                    def _(h=h, d=d, j=j):
                        behind_copy(h, d, j).wait_send()

                ahead_wait(d, h)
            behind_wait(d, o)

    @pl.when(inner == 0)
    def _():
        feeder()

    @pl.when(inner == 1)
    def _():
        worker()


def shards(n, reps, coords, frame_count):
    atoms, frames = coords.shape[1], coords.shape[2]
    half = frames // 2
    pitch = (atoms + 15) // 16 * 16
    again = (2 * pitch + 127) // 128 * 128
    depth = again + (pitch + 127) // 128 * 128
    f32, bf16 = jnp.float32, jnp.bfloat16
    dma = pltpu.SemaphoreType.DMA
    vmem = pl.BlockSpec(memory_space=pltpu.VMEM)
    result = jax.ShapeDtypeStruct((ROUNDS, frames // reps, frames), f32)
    return pl.pallas_call(
        functools.partial(kernel, n, reps),
        out_shape=(result, result),
        in_specs=[pl.BlockSpec(memory_space=pl.ANY), pl.BlockSpec(memory_space=pltpu.SMEM)],
        out_specs=(vmem, vmem),
        scratch_shapes=[
            pltpu.VMEM((reps, 2, 3, atoms, half), f32),
            pltpu.VMEM((ROUNDS, reps, 3, atoms, half), f32),
            pltpu.VMEM((8, half), jnp.int32),
            pltpu.VMEM((ROUNDS, 8, half), jnp.int32),
            pltpu.VMEM((again, half), f32),
            pltpu.VMEM((2, reps, 3 * half, depth), bf16),
            pltpu.VMEM((reps, depth, ROUNDS * 3 * half), bf16),
            pltpu.VMEM((2, 3 * half, ROUNDS * 3 * half), f32),
            pltpu.VMEM((2, 3, 8, half), f32),
            pltpu.VMEM((2, 4, 8, half), f32),
            pltpu.VMEM((ROUNDS, 3, 8, half), f32),
            pltpu.VMEM((ROUNDS, 4, 8, half), f32),
            pltpu.VMEM((4, half, half), f32),
            pltpu.VMEM((2, ROUNDS, half, half), f32),
            pltpu.VMEM((2, ROUNDS, half, half), f32),
            dma((2, 2, 3)),
            dma((reps, 2, 3)),
            dma((ROUNDS, 3)),
            dma((4, reps, 3)),
            dma((ROUNDS, reps, 3)),
            dma((4,)),
            dma((ROUNDS,)),
            dma((2, ROUNDS, 4)),
            dma((ROUNDS, 2)),
            dma((ROUNDS, 2)),
            dma((2,)),
            pltpu.SemaphoreType.REGULAR,
        ],
        compiler_params=pltpu.CompilerParams(collective_id=0, has_side_effects=True,
                                             vmem_limit_bytes=48 * 1024 * 1024),
    )(coords, frame_count.astype(jnp.int32))


def solution(mesh):
    in_specs = (P(None, "rep", "blk"), P("blk"))
    out_specs = (P(None, ("blk", "rep"), None), P(None, ("blk", "rep"), None))
    body = functools.partial(shards, mesh.shape["blk"], mesh.shape["rep"])
    return jax.shard_map(body, mesh=mesh, in_specs=in_specs, out_specs=out_specs, check_vma=False)
```

```python
import functools

import jax
import jax.numpy as jnp
from jax import lax
from jax.experimental import pallas as pl
from jax.experimental.pallas import tpu as pltpu
from jax.sharding import PartitionSpec as P

ROUNDS = 3
NEWTON = 4
MESH = pl.DeviceIdType.MESH


def pair_minor(upper, lower, left, right):
    return upper[left] * lower[right] - upper[right] * lower[left]


def deviation(m, total):
    keyed = [
        [m[0][0] + m[1][1] + m[2][2], m[1][2] - m[2][1], m[2][0] - m[0][2], m[0][1] - m[1][0]],
        [m[1][2] - m[2][1], m[0][0] - m[1][1] - m[2][2], m[0][1] + m[1][0], m[2][0] + m[0][2]],
        [m[2][0] - m[0][2], m[0][1] + m[1][0], -m[0][0] + m[1][1] - m[2][2], m[1][2] + m[2][1]],
        [m[0][1] - m[1][0], m[2][0] + m[0][2], m[1][2] + m[2][1], -m[0][0] - m[1][1] + m[2][2]],
    ]
    top_one, top_two, low_one, low_two = keyed
    det_key = (
        pair_minor(top_one, top_two, 0, 1) * pair_minor(low_one, low_two, 2, 3)
        - pair_minor(top_one, top_two, 0, 2) * pair_minor(low_one, low_two, 1, 3)
        + pair_minor(top_one, top_two, 0, 3) * pair_minor(low_one, low_two, 1, 2)
        + pair_minor(top_one, top_two, 1, 2) * pair_minor(low_one, low_two, 0, 3)
        - pair_minor(top_one, top_two, 1, 3) * pair_minor(low_one, low_two, 0, 2)
        + pair_minor(top_one, top_two, 2, 3) * pair_minor(low_one, low_two, 0, 1)
    )
    det_three = (
        m[0][0] * (m[1][1] * m[2][2] - m[1][2] * m[2][1])
        - m[0][1] * (m[1][0] * m[2][2] - m[1][2] * m[2][0])
        + m[0][2] * (m[1][0] * m[2][1] - m[1][1] * m[2][0])
    )
    square_sum = m[0][0] * m[0][0]
    for first in range(3):
        for second in range(3):
            if first + second > 0:
                square_sum = square_sum + m[first][second] * m[first][second]
    second_coef = -2.0 * square_sum
    first_coef = -8.0 * det_three
    largest = 0.5 * total
    for newton_step in range(NEWTON):
        squared = largest * largest
        polynomial = squared * squared + second_coef * squared + first_coef * largest + det_key
        derivative = 4.0 * squared * largest + 2.0 * second_coef * largest + first_coef
        largest = largest - polynomial / derivative
    return total - 2.0 * largest


def split(value):
    high = value.astype(jnp.bfloat16)
    low = (value - high.astype(jnp.float32)).astype(jnp.bfloat16)
    return high, low


def kernel(n, reps, coords, count, behind, ahead, own, part, cnt, pcnt, full, ft, gt, cov,
           fshift, fsum, gshift, gsum, col, dev, devt,
           zs, zr, fs, xs, pr, cs, cr, os, br, ar, ls, go):
    b = lax.axis_index("blk")
    z = lax.axis_index("rep")
    par = lax.rem(b, 2)
    odd = lax.rem(b // 2, 2)
    bent = odd * par == 1
    bends = odd * (1 - par) == 1
    atoms = coords.shape[1]
    half = coords.shape[2] // 2
    quarter = half // 2
    natom = atoms * reps
    pitch = (atoms + 15) // 16 * 16
    again = full.shape[0]
    tail = ft.shape[3] - again
    g = z // 2
    o = 1 - g
    me = z
    fd = (reps - 1) * g
    of = reps - 1 - fd
    ot = reps - 1 - z
    wk = 1 + g
    inner = jnp.minimum(z, 1) * jnp.minimum(reps - 1 - z, 1)

    def at(step):
        return lax.rem(b + step + n, n)

    barrier = pltpu.get_barrier_semaphore()
    for step in (1 - 2 * par, 2 - 4 * odd, 6 * par - 3):
        pl.semaphore_signal(barrier, inc=1, device_id=(at(step), z), device_id_type=MESH)

    @pl.when(odd + par == 1)
    def _():
        pl.semaphore_signal(barrier, inc=1, device_id=(at(1 - 2 * odd), z), device_id_type=MESH)

    @pl.when(z > 0)
    def _():
        pl.semaphore_signal(barrier, inc=1, device_id=(b, z - 1), device_id_type=MESH)

    @pl.when(z < reps - 1)
    def _():
        pl.semaphore_signal(barrier, inc=1, device_id=(b, z + 1), device_id_type=MESH)

    pl.semaphore_wait(barrier, 4 + lax.rem(odd + par, 2) + inner)

    @pl.when((odd == 0) & (par == 1))
    def _():
        pl.semaphore_signal(go, inc=1, device_id=(at(1), z), device_id_type=MESH)

    def remote(src, dst, send, recv, where):
        return pltpu.make_async_remote_copy(src_ref=src, dst_ref=dst, send_sem=send, recv_sem=recv,
                                            device_id=where, device_id_type=MESH)

    def lanes(h):
        return pl.ds(pl.multiple_of(h * half, half), half)

    def source(s, h, k, mine):
        return coords.at[k, :, lanes(h)] if mine else own.at[s, h, k]

    def along(s, h, k, mine, where):
        return remote(source(s, h, k, mine), own.at[s, h, k], zs.at[1 - mine, h, k], zr.at[s, h, k],
                      (b, where))

    def first(s, k, mine):
        slot = 2 * par
        return remote(source(s, g, k, mine), part.at[slot, s, k], xs.at[1, s, k], pr.at[slot, s, k],
                      (at(1 + slot), z))

    def second(s, k, mine):
        return remote(source(s, g, k, mine), part.at[1, s, k], xs.at[0, s, k], pr.at[1, s, k],
                      (at(2), z))

    def bend(s, k):
        return remote(part.at[2, s, k], part.at[1, s, k], xs.at[3, s, k], pr.at[1, s, k],
                      (at(-1), z))

    def relay(s, k):
        slot = 2 - 2 * par
        return remote(part.at[1, s, k], part.at[slot, s, k], xs.at[2, s, k], pr.at[slot, s, k],
                      (at(1 - 2 * par), z))

    def feed(slot, k):
        return remote(part.at[slot, z, k], part.at[slot, z, k], fs.at[slot, k], pr.at[slot, z, k],
                      (b, wk))

    def count_first():
        slot = 2 * par
        return remote(cnt, pcnt.at[slot], cs.at[1], cr.at[slot], (at(1 + slot), z))

    def count_second():
        return remote(cnt, pcnt.at[1], cs.at[0], cr.at[1], (at(2), z))

    def count_bend():
        return remote(pcnt.at[2], pcnt.at[1], cs.at[3], cr.at[1], (at(-1), z))

    def count_relay():
        slot = 2 - 2 * par
        return remote(pcnt.at[1], pcnt.at[slot], cs.at[2], cr.at[slot], (at(1 - 2 * par), z))

    def zr_wait(s, h, k):
        remote(own.at[s, h, k], own.at[s, h, k], zs.at[0, h, k], zr.at[s, h, k],
               (b, lax.rem(z + 1, reps))).wait_recv()

    def pr_wait(d, s, k):
        remote(part.at[d, s, k], part.at[d, s, k], xs.at[0, s, k], pr.at[d, s, k],
               (b, lax.rem(z + 1, reps))).wait_recv()

    def cr_wait(d):
        remote(pcnt.at[d], pcnt.at[d], cs.at[0], cr.at[d], (b, lax.rem(z + 1, reps))).wait_recv()

    def local(h):
        return pltpu.make_async_copy(coords.at[:, :, lanes(h)], own.at[z, h], ls.at[h])

    def behind_copy(h, d, j):
        return remote(dev.at[h, d, pl.ds(j * quarter, quarter)], behind.at[d, :, lanes(g)],
                      os.at[h, d, 2 + j], br.at[d, g], (b, 2 * h + j))

    def ahead_copy(h, d, j):
        return remote(devt.at[h, d, pl.ds(j * quarter, quarter)], ahead.at[d, :, lanes(h)],
                      os.at[h, d, j], ar.at[d, h], (lax.rem(b - 1 - d + n, n), 2 * g + j))

    def ahead_wait(d, h):
        remote(devt.at[0, d, pl.ds(0, quarter)], ahead.at[d, :, pl.ds(h * half, half)],
               os.at[0, d, 0], ar.at[d, h], (at(1), z)).wait_recv()

    def behind_wait(d, side):
        remote(dev.at[0, d, pl.ds(0, quarter)], behind.at[d, :, lanes(side)],
               os.at[0, d, 2], br.at[d, side], (at(1), z)).wait_recv()

    def feeder():
        for k in range(3):
            along(me, o, k, True, wk).start()

            @pl.when(par == 1)
            def _(k=k):
                first(me, k, True).start()

        @pl.when(bends)
        def _():
            pl.semaphore_wait(go, 1)

        for k in range(3):
            @pl.when(jnp.logical_not(bent))
            def _(k=k):
                second(me, k, True).start()

        for k in range(3):
            along(me, g, k, True, wk).start()
        for k in range(3):
            @pl.when(par == 0)
            def _(k=k):
                pr_wait(2, me, k)

                @pl.when(bends)
                def _():
                    bend(me, k).start()

                feed(2, k).start()

        for k in range(3):
            pr_wait(1, me, k)
            feed(1, k).start()
        for k in range(3):
            along(me, o, k, True, wk).wait_send()
            along(me, g, k, True, wk).wait_send()
            feed(1, k).wait_send()

            @pl.when(par == 0)
            def _(k=k):
                feed(2, k).wait_send()

            @pl.when(par == 1)
            def _(k=k):
                first(me, k, True).wait_send()

            @pl.when(jnp.logical_not(bent))
            def _(k=k):
                second(me, k, True).wait_send()

            @pl.when(bends)
            def _(k=k):
                bend(me, k).wait_send()

        for d in range(ROUNDS):
            for side in range(2):
                behind_wait(d, side)
                ahead_wait(d, side)

    def across(s, k, mine):
        first(s, k, mine).start()

        @pl.when(jnp.logical_not(bent))
        def _():
            second(s, k, mine).start()

    def turn(s, k):
        @pl.when(bends)
        def _():
            pr_wait(2, s, k)
            bend(s, k).start()

    def pass_on(s, k):
        pr_wait(1, s, k)
        relay(s, k).start()

    def settle(s, bent_in):
        for k in range(3):
            pr_wait(0, s, k)

            if bent_in:
                @pl.when(jnp.logical_not(bends))
                def _(k=k):
                    pr_wait(2, s, k)
            else:
                pr_wait(2, s, k)

    def own_part(s, h, k, start):
        value = own[s, h, k]
        if start:
            shift = jnp.sum(value, axis=0, keepdims=True) / atoms
            fshift[h, k, 0:1, :] = shift
        else:
            shift = fshift[h, k, 0:1, :]
        value = value - shift
        total = jnp.sum(value, axis=0, keepdims=True)
        square = jnp.sum(value * value, axis=0, keepdims=True)
        fsum[h, k, 0:1, :] = fsum[h, k, 0:1, :] + total
        fsum[h, 3, 0:1, :] = fsum[h, 3, 0:1, :] + square
        high = value.astype(jnp.bfloat16).astype(jnp.float32)
        full[0:atoms, :] = high
        full[pitch:pitch + atoms, :] = value - high
        turned = full[...].T.astype(jnp.bfloat16)
        ft[h, s, k * half:(k + 1) * half, 0:again] = turned
        ft[h, s, k * half:(k + 1) * half, again:again + tail] = turned[:, 0:tail]

    def partner_part(s, start):
        for d in range(ROUNDS):
            for k in range(3):
                value = part[d, s, k]
                if start:
                    shift = jnp.sum(value, axis=0, keepdims=True) / atoms
                    gshift[d, k, 0:1, :] = shift
                else:
                    shift = gshift[d, k, 0:1, :]
                value = value - shift
                total = jnp.sum(value, axis=0, keepdims=True)
                square = jnp.sum(value * value, axis=0, keepdims=True)
                gsum[d, k, 0:1, :] = gsum[d, k, 0:1, :] + total
                gsum[d, 3, 0:1, :] = gsum[d, 3, 0:1, :] + square
                high, low = split(value)
                place = slice((3 * d + k) * half, (3 * d + k + 1) * half)
                gt[s, 0:atoms, place] = high
                gt[s, pitch:pitch + atoms, place] = high
                gt[s, again:again + atoms, place] = low

    product = functools.partial(jnp.dot, preferred_element_type=jnp.float32)

    def multiply(s, h, start=False):
        term = product(ft[h, s], gt[s])
        cov[h] = term if start else cov[h] + term

    def multiply_rows(s, h, k):
        rows = slice(k * half, (k + 1) * half)
        cov[h, rows, :] = cov[h, rows, :] + product(ft[h, s, rows, :], gt[s])

    def tile(h):
        square = fsum[h, 3, 0:1, :] / natom
        for k in range(3):
            mean = fsum[h, k, 0:1, :] / natom
            square = square - mean * mean
            col[k] = jnp.broadcast_to(mean, (half, half)).T
        col[3] = jnp.broadcast_to(square, (half, half)).T
        rows = half // 4

        def block(d, carry):
            mean = [gsum[d, k, 0:1, :] / natom for k in range(3)]
            other_square = gsum[d, 3, 0:1, :] / natom
            for k in range(3):
                other_square = other_square - mean[k] * mean[k]

            def chunk(i, inner_carry):
                r = pl.multiple_of(i * rows, rows)
                m = [[cov[h, pl.ds(k * half + r, rows), lanes(3 * d + l)] * (1.0 / natom)
                      - col[k, pl.ds(r, rows), :] * mean[l] for l in range(3)] for k in range(3)]
                total = col[3, pl.ds(r, rows), :] + other_square
                frame = h * half + r + lax.broadcasted_iota(jnp.int32, (rows, half), 0)
                other = g * half + lax.broadcasted_iota(jnp.int32, (rows, half), 1)
                mask = (frame < cnt[0:1, :]) & (other < pcnt[d, 0:1, :])
                dev[h, d, pl.ds(r, rows), :] = jnp.where(mask, deviation(m, total), 0.0)
                return inner_carry

            lax.fori_loop(0, half // rows, chunk, 0)
            for j in range(2):
                @pl.when(2 * h + j != z)
                def _(j=j):
                    behind_copy(h, d, j).start()

                @pl.when(2 * h + j == z)
                def _(j=j):
                    behind[d, :, lanes(g)] = dev[h, d, j * quarter:(j + 1) * quarter, :]

            devt[h, d] = dev[h, d].T
            for j in range(2):
                ahead_copy(h, d, j).start()
            return carry

        lax.fori_loop(0, ROUNDS, block, 0)

    def worker():
        for k in range(3):
            along(me, o, k, True, ot).start()
            first(me, k, True).start()

        @pl.when(bends)
        def _():
            pl.semaphore_wait(go, 1)

        for k in range(3):
            @pl.when(jnp.logical_not(bent))
            def _(k=k):
                second(me, k, True).start()

        for h in range(2):
            local(h).start()
        cnt[...] = jnp.full(cnt.shape, count[0], jnp.int32)
        count_first().start()

        @pl.when(jnp.logical_not(bent))
        def _():
            count_second().start()

        full[...] = jnp.zeros_like(full)
        fsum[...] = jnp.zeros_like(fsum)
        gsum[...] = jnp.zeros_like(gsum)
        for h in range(2):
            local(h).wait()
        for k in range(3):
            own_part(me, g, k, True)
        for k in range(3):
            zr_wait(fd, o, k)
            along(fd, o, k, False, ot).start()
            zr_wait(ot, g, k)
            across(ot, k, False)
            turn(me, k)
            own_part(me, o, k, True)
            if k == 1:
                along(me, g, 0, True, ot).start()

        @pl.when(bends)
        def _():
            cr_wait(2)
            count_bend().start()

        for k in range(1, 3):
            along(me, g, k, True, ot).start()
        gt[...] = jnp.zeros_like(gt)
        for k in range(3):
            pass_on(me, k)
        cr_wait(1)
        count_relay().start()
        settle(me, True)
        partner_part(me, True)
        for h in range(2):
            multiply(me, h, True)
        for k in range(3):
            own_part(ot, g, k, False)
            zr_wait(fd, g, k)
            along(fd, g, k, False, ot).start()

            @pl.when(par == 0)
            def _(k=k):
                first(fd, k, False).start()

            turn(ot, k)
            zr_wait(of, g, k)
            across(of, k, False)
            own_part(fd, o, k, False)
        for k in range(3):
            pass_on(ot, k)
        settle(ot, True)
        partner_part(ot, False)
        multiply(ot, g)
        for k in range(3):
            turn(of, k)
            own_part(fd, g, k, False)
            own_part(of, g, k, False)
        for k in range(3):
            zr_wait(ot, o, k)
            own_part(ot, o, k, False)
        multiply(ot, o)
        for k in range(3):
            pass_on(of, k)
        settle(of, True)
        partner_part(of, False)
        multiply(of, g)
        for k in range(3):
            pass_on(fd, k)
        for k in range(3):
            pr_wait(0, fd, k)
            pr_wait(2, fd, k)
        partner_part(fd, False)
        for h in range(2):
            multiply(fd, h)
        cr_wait(0)

        @pl.when(jnp.logical_not(bends))
        def _():
            cr_wait(2)

        tile(g)
        for k in range(3):
            zr_wait(of, o, k)
            own_part(of, o, k, False)
            multiply_rows(of, o, k)
        tile(o)
        finish()

    def finish():
        for k in range(3):
            for h in range(2):
                along(me, h, k, True, ot).wait_send()
                along(fd, h, k, False, ot).wait_send()
            for s in (me, ot, of):
                first(s, k, False).wait_send()
                relay(s, k).wait_send()

                @pl.when(jnp.logical_not(bent))
                def _(s=s, k=k):
                    second(s, k, False).wait_send()

                @pl.when(bends)
                def _(s=s, k=k):
                    bend(s, k).wait_send()

            relay(fd, k).wait_send()

            @pl.when(par == 0)
            def _(k=k):
                first(fd, k, False).wait_send()

        count_first().wait_send()
        count_relay().wait_send()

        @pl.when(jnp.logical_not(bent))
        def _():
            count_second().wait_send()

        @pl.when(bends)
        def _():
            count_bend().wait_send()

        for d in range(ROUNDS):
            for h in range(2):
                for j in range(2):
                    ahead_copy(h, d, j).wait_send()

                    @pl.when(2 * h + j != z)
                    def _(h=h, d=d, j=j):
                        behind_copy(h, d, j).wait_send()

                ahead_wait(d, h)
            behind_wait(d, o)

    @pl.when(inner == 0)
    def _():
        feeder()

    @pl.when(inner == 1)
    def _():
        worker()


def shards(n, reps, coords, frame_count):
    atoms, frames = coords.shape[1], coords.shape[2]
    half = frames // 2
    pitch = (atoms + 15) // 16 * 16
    again = (2 * pitch + 127) // 128 * 128
    depth = again + (pitch + 127) // 128 * 128
    f32, bf16 = jnp.float32, jnp.bfloat16
    dma = pltpu.SemaphoreType.DMA
    vmem = pl.BlockSpec(memory_space=pltpu.VMEM)
    result = jax.ShapeDtypeStruct((ROUNDS, frames // reps, frames), f32)
    return pl.pallas_call(
        functools.partial(kernel, n, reps),
        out_shape=(result, result),
        in_specs=[pl.BlockSpec(memory_space=pl.ANY), pl.BlockSpec(memory_space=pltpu.SMEM)],
        out_specs=(vmem, vmem),
        scratch_shapes=[
            pltpu.VMEM((reps, 2, 3, atoms, half), f32),
            pltpu.VMEM((ROUNDS, reps, 3, atoms, half), f32),
            pltpu.VMEM((8, half), jnp.int32),
            pltpu.VMEM((ROUNDS, 8, half), jnp.int32),
            pltpu.VMEM((again, half), f32),
            pltpu.VMEM((2, reps, 3 * half, depth), bf16),
            pltpu.VMEM((reps, depth, ROUNDS * 3 * half), bf16),
            pltpu.VMEM((2, 3 * half, ROUNDS * 3 * half), f32),
            pltpu.VMEM((2, 3, 8, half), f32),
            pltpu.VMEM((2, 4, 8, half), f32),
            pltpu.VMEM((ROUNDS, 3, 8, half), f32),
            pltpu.VMEM((ROUNDS, 4, 8, half), f32),
            pltpu.VMEM((4, half, half), f32),
            pltpu.VMEM((2, ROUNDS, half, half), f32),
            pltpu.VMEM((2, ROUNDS, half, half), f32),
            dma((2, 2, 3)),
            dma((reps, 2, 3)),
            dma((ROUNDS, 3)),
            dma((4, reps, 3)),
            dma((ROUNDS, reps, 3)),
            dma((4,)),
            dma((ROUNDS,)),
            dma((2, ROUNDS, 4)),
            dma((ROUNDS, 2)),
            dma((ROUNDS, 2)),
            dma((2,)),
            pltpu.SemaphoreType.REGULAR,
        ],
        compiler_params=pltpu.CompilerParams(collective_id=0, has_side_effects=True,
                                             vmem_limit_bytes=53 * 1024 * 1024),
    )(coords, frame_count.astype(jnp.int32))


def solution(mesh):
    in_specs = (P(None, "rep", "blk"), P("blk"))
    out_specs = (P(None, ("blk", "rep"), None), P(None, ("blk", "rep"), None))
    body = functools.partial(shards, mesh.shape["blk"], mesh.shape["rep"])
    return jax.shard_map(body, mesh=mesh, in_specs=in_specs, out_specs=out_specs, check_vma=False)
```

```python
import functools

import jax
import jax.numpy as jnp
from jax import lax
from jax.experimental import pallas as pl
from jax.experimental.pallas import tpu as pltpu
from jax.sharding import PartitionSpec as P

ROUNDS = 3
NEWTON = 4
MESH = pl.DeviceIdType.MESH


def pair_minor(upper, lower, left, right):
    return upper[left] * lower[right] - upper[right] * lower[left]


def deviation(m, total):
    keyed = [
        [m[0][0] + m[1][1] + m[2][2], m[1][2] - m[2][1], m[2][0] - m[0][2], m[0][1] - m[1][0]],
        [m[1][2] - m[2][1], m[0][0] - m[1][1] - m[2][2], m[0][1] + m[1][0], m[2][0] + m[0][2]],
        [m[2][0] - m[0][2], m[0][1] + m[1][0], -m[0][0] + m[1][1] - m[2][2], m[1][2] + m[2][1]],
        [m[0][1] - m[1][0], m[2][0] + m[0][2], m[1][2] + m[2][1], -m[0][0] - m[1][1] + m[2][2]],
    ]
    top_one, top_two, low_one, low_two = keyed
    det_key = (
        pair_minor(top_one, top_two, 0, 1) * pair_minor(low_one, low_two, 2, 3)
        - pair_minor(top_one, top_two, 0, 2) * pair_minor(low_one, low_two, 1, 3)
        + pair_minor(top_one, top_two, 0, 3) * pair_minor(low_one, low_two, 1, 2)
        + pair_minor(top_one, top_two, 1, 2) * pair_minor(low_one, low_two, 0, 3)
        - pair_minor(top_one, top_two, 1, 3) * pair_minor(low_one, low_two, 0, 2)
        + pair_minor(top_one, top_two, 2, 3) * pair_minor(low_one, low_two, 0, 1)
    )
    det_three = (
        m[0][0] * (m[1][1] * m[2][2] - m[1][2] * m[2][1])
        - m[0][1] * (m[1][0] * m[2][2] - m[1][2] * m[2][0])
        + m[0][2] * (m[1][0] * m[2][1] - m[1][1] * m[2][0])
    )
    square_sum = m[0][0] * m[0][0]
    for first in range(3):
        for second in range(3):
            if first + second > 0:
                square_sum = square_sum + m[first][second] * m[first][second]
    second_coef = -2.0 * square_sum
    first_coef = -8.0 * det_three
    largest = 0.5 * total
    for newton_step in range(NEWTON):
        squared = largest * largest
        polynomial = squared * squared + second_coef * squared + first_coef * largest + det_key
        derivative = 4.0 * squared * largest + 2.0 * second_coef * largest + first_coef
        largest = largest - polynomial / derivative
    return total - 2.0 * largest


def split(value):
    high = value.astype(jnp.bfloat16)
    low = (value - high.astype(jnp.float32)).astype(jnp.bfloat16)
    return high, low


def kernel(n, reps, coords, count, behind, ahead, own, part, cnt, pcnt, full, ft, gt, cov,
           fshift, fsum, gshift, gsum, col, dev, devt,
           zs, zr, fs, xs, pr, cs, cr, os, br, ar, ls, go):
    b = lax.axis_index("blk")
    z = lax.axis_index("rep")
    par = lax.rem(b, 2)
    odd = lax.rem(b // 2, 2)
    bent = odd * par == 1
    bends = odd * (1 - par) == 1
    atoms = coords.shape[1]
    half = coords.shape[2] // 2
    quarter = half // 2
    natom = atoms * reps
    pitch = (atoms + 15) // 16 * 16
    again = full.shape[0]
    tail = ft.shape[3] - again
    g = z // 2
    o = 1 - g
    me = z
    fd = (reps - 1) * g
    of = reps - 1 - fd
    ot = reps - 1 - z
    wk = 1 + g
    inner = jnp.minimum(z, 1) * jnp.minimum(reps - 1 - z, 1)

    def at(step):
        return lax.rem(b + step + n, n)

    barrier = pltpu.get_barrier_semaphore()
    for step in (1 - 2 * par, 2 - 4 * odd, 6 * par - 3):
        pl.semaphore_signal(barrier, inc=1, device_id=(at(step), z), device_id_type=MESH)

    @pl.when(odd + par == 1)
    def _():
        pl.semaphore_signal(barrier, inc=1, device_id=(at(1 - 2 * odd), z), device_id_type=MESH)

    @pl.when(z > 0)
    def _():
        pl.semaphore_signal(barrier, inc=1, device_id=(b, z - 1), device_id_type=MESH)

    @pl.when(z < reps - 1)
    def _():
        pl.semaphore_signal(barrier, inc=1, device_id=(b, z + 1), device_id_type=MESH)

    pl.semaphore_wait(barrier, 4 + lax.rem(odd + par, 2) + inner)

    @pl.when((odd == 0) & (par == 1))
    def _():
        pl.semaphore_signal(go, inc=1, device_id=(at(1), z), device_id_type=MESH)

    def remote(src, dst, send, recv, where):
        return pltpu.make_async_remote_copy(src_ref=src, dst_ref=dst, send_sem=send, recv_sem=recv,
                                            device_id=where, device_id_type=MESH)

    def lanes(h):
        return pl.ds(pl.multiple_of(h * half, half), half)

    def source(s, h, k, mine):
        return coords.at[k, :, lanes(h)] if mine else own.at[s, h, k]

    def along(s, h, k, mine, where):
        return remote(source(s, h, k, mine), own.at[s, h, k], zs.at[1 - mine, h, k], zr.at[s, h, k],
                      (b, where))

    def first(s, k, mine):
        slot = 2 * par
        return remote(source(s, g, k, mine), part.at[slot, s, k], xs.at[1, s, k], pr.at[slot, s, k],
                      (at(1 + slot), z))

    def second(s, k, mine):
        return remote(source(s, g, k, mine), part.at[1, s, k], xs.at[0, s, k], pr.at[1, s, k],
                      (at(2), z))

    def bend(s, k):
        return remote(part.at[2, s, k], part.at[1, s, k], xs.at[3, s, k], pr.at[1, s, k],
                      (at(-1), z))

    def relay(s, k):
        slot = 2 - 2 * par
        return remote(part.at[1, s, k], part.at[slot, s, k], xs.at[2, s, k], pr.at[slot, s, k],
                      (at(1 - 2 * par), z))

    def feed(k):
        return remote(part.at[1, z, k], part.at[1, z, k], fs.at[k], pr.at[1, z, k], (b, wk))

    def count_first():
        slot = 2 * par
        return remote(cnt, pcnt.at[slot], cs.at[1], cr.at[slot], (at(1 + slot), z))

    def count_second():
        return remote(cnt, pcnt.at[1], cs.at[0], cr.at[1], (at(2), z))

    def count_bend():
        return remote(pcnt.at[2], pcnt.at[1], cs.at[3], cr.at[1], (at(-1), z))

    def count_relay():
        slot = 2 - 2 * par
        return remote(pcnt.at[1], pcnt.at[slot], cs.at[2], cr.at[slot], (at(1 - 2 * par), z))

    def zr_wait(s, h, k):
        remote(own.at[s, h, k], own.at[s, h, k], zs.at[0, h, k], zr.at[s, h, k],
               (b, lax.rem(z + 1, reps))).wait_recv()

    def pr_wait(d, s, k):
        remote(part.at[d, s, k], part.at[d, s, k], xs.at[0, s, k], pr.at[d, s, k],
               (b, lax.rem(z + 1, reps))).wait_recv()

    def cr_wait(d):
        remote(pcnt.at[d], pcnt.at[d], cs.at[0], cr.at[d], (b, lax.rem(z + 1, reps))).wait_recv()

    def local(h):
        return pltpu.make_async_copy(coords.at[:, :, lanes(h)], own.at[z, h], ls.at[h])

    def behind_copy(h, d, j):
        return remote(dev.at[h, d, pl.ds(j * quarter, quarter)], behind.at[d, :, lanes(g)],
                      os.at[h, d, 2 + j], br.at[d, g], (b, 2 * h + j))

    def ahead_copy(h, d, j):
        return remote(devt.at[h, d, pl.ds(j * quarter, quarter)], ahead.at[d, :, lanes(h)],
                      os.at[h, d, j], ar.at[d, h], (lax.rem(b - 1 - d + n, n), 2 * g + j))

    def ahead_wait(d, h):
        remote(devt.at[0, d, pl.ds(0, quarter)], ahead.at[d, :, pl.ds(h * half, half)],
               os.at[0, d, 0], ar.at[d, h], (at(1), z)).wait_recv()

    def behind_wait(d, side):
        remote(dev.at[0, d, pl.ds(0, quarter)], behind.at[d, :, lanes(side)],
               os.at[0, d, 2], br.at[d, side], (at(1), z)).wait_recv()

    def feeder():
        for k in range(3):
            along(me, o, k, True, wk).start()

            @pl.when(bent)
            def _(k=k):
                first(me, k, True).start()

        @pl.when(bends)
        def _():
            pl.semaphore_wait(go, 1)

        for k in range(3):
            @pl.when(jnp.logical_not(bent))
            def _(k=k):
                second(me, k, True).start()

        for k in range(3):
            along(me, g, k, True, wk).start()
        for k in range(3):
            turn(me, k)
        for k in range(3):
            pr_wait(1, me, k)
            feed(k).start()
        for k in range(3):
            along(me, o, k, True, wk).wait_send()
            along(me, g, k, True, wk).wait_send()
            feed(k).wait_send()

            @pl.when(bent)
            def _(k=k):
                first(me, k, True).wait_send()

            @pl.when(jnp.logical_not(bent))
            def _(k=k):
                second(me, k, True).wait_send()

            @pl.when(bends)
            def _(k=k):
                bend(me, k).wait_send()

        for d in range(ROUNDS):
            for side in range(2):
                behind_wait(d, side)
                ahead_wait(d, side)

    def across(s, k, mine):
        first(s, k, mine).start()

        @pl.when(jnp.logical_not(bent))
        def _():
            second(s, k, mine).start()

    def turn(s, k):
        @pl.when(bends)
        def _():
            pr_wait(2, s, k)
            bend(s, k).start()

    def pass_on(s, k):
        pr_wait(1, s, k)
        relay(s, k).start()

    def settle(s, bent_in):
        for k in range(3):
            pr_wait(0, s, k)

            if bent_in:
                @pl.when(jnp.logical_not(bends))
                def _(k=k):
                    pr_wait(2, s, k)
            else:
                pr_wait(2, s, k)

    def own_part(s, h, k, start):
        value = own[s, h, k]
        if start:
            shift = jnp.sum(value, axis=0, keepdims=True) / atoms
            fshift[h, k, 0:1, :] = shift
        else:
            shift = fshift[h, k, 0:1, :]
        value = value - shift
        total = jnp.sum(value, axis=0, keepdims=True)
        square = jnp.sum(value * value, axis=0, keepdims=True)
        fsum[h, k, 0:1, :] = fsum[h, k, 0:1, :] + total
        fsum[h, 3, 0:1, :] = fsum[h, 3, 0:1, :] + square
        high = value.astype(jnp.bfloat16).astype(jnp.float32)
        full[0:atoms, :] = high
        full[pitch:pitch + atoms, :] = value - high
        turned = full[...].T.astype(jnp.bfloat16)
        ft[h, s, k * half:(k + 1) * half, 0:again] = turned
        ft[h, s, k * half:(k + 1) * half, again:again + tail] = turned[:, 0:tail]

    def partner_part(s, start):
        for d in range(ROUNDS):
            for k in range(3):
                value = part[d, s, k]
                if start:
                    shift = jnp.sum(value, axis=0, keepdims=True) / atoms
                    gshift[d, k, 0:1, :] = shift
                else:
                    shift = gshift[d, k, 0:1, :]
                value = value - shift
                total = jnp.sum(value, axis=0, keepdims=True)
                square = jnp.sum(value * value, axis=0, keepdims=True)
                gsum[d, k, 0:1, :] = gsum[d, k, 0:1, :] + total
                gsum[d, 3, 0:1, :] = gsum[d, 3, 0:1, :] + square
                high, low = split(value)
                place = slice((3 * d + k) * half, (3 * d + k + 1) * half)
                gt[s, 0:atoms, place] = high
                gt[s, pitch:pitch + atoms, place] = high
                gt[s, again:again + atoms, place] = low

    product = functools.partial(jnp.dot, preferred_element_type=jnp.float32)

    def multiply(s, h, start=False):
        term = product(ft[h, s], gt[s])
        cov[h] = term if start else cov[h] + term

    def multiply_rows(s, h, k):
        rows = slice(k * half, (k + 1) * half)
        cov[h, rows, :] = cov[h, rows, :] + product(ft[h, s, rows, :], gt[s])

    def tile(h):
        square = fsum[h, 3, 0:1, :] / natom
        for k in range(3):
            mean = fsum[h, k, 0:1, :] / natom
            square = square - mean * mean
            col[k] = jnp.broadcast_to(mean, (half, half)).T
        col[3] = jnp.broadcast_to(square, (half, half)).T
        rows = half // 4

        def block(d, carry):
            mean = [gsum[d, k, 0:1, :] / natom for k in range(3)]
            other_square = gsum[d, 3, 0:1, :] / natom
            for k in range(3):
                other_square = other_square - mean[k] * mean[k]

            def chunk(i, inner_carry):
                r = pl.multiple_of(i * rows, rows)
                m = [[cov[h, pl.ds(k * half + r, rows), lanes(3 * d + l)] * (1.0 / natom)
                      - col[k, pl.ds(r, rows), :] * mean[l] for l in range(3)] for k in range(3)]
                total = col[3, pl.ds(r, rows), :] + other_square
                frame = h * half + r + lax.broadcasted_iota(jnp.int32, (rows, half), 0)
                other = g * half + lax.broadcasted_iota(jnp.int32, (rows, half), 1)
                mask = (frame < cnt[0:1, :]) & (other < pcnt[d, 0:1, :])
                dev[h, d, pl.ds(r, rows), :] = jnp.where(mask, deviation(m, total), 0.0)
                return inner_carry

            lax.fori_loop(0, half // rows, chunk, 0, unroll=True)
            for j in range(2):
                @pl.when(2 * h + j != z)
                def _(j=j):
                    behind_copy(h, d, j).start()

                @pl.when(2 * h + j == z)
                def _(j=j):
                    behind[d, :, lanes(g)] = dev[h, d, j * quarter:(j + 1) * quarter, :]

            devt[h, d] = dev[h, d].T
            for j in range(2):
                ahead_copy(h, d, j).start()
            return carry

        lax.fori_loop(0, ROUNDS, block, 0)

    def worker():
        for k in range(3):
            along(me, o, k, True, ot).start()
            first(me, k, True).start()

        @pl.when(bends)
        def _():
            pl.semaphore_wait(go, 1)

        for k in range(3):
            @pl.when(jnp.logical_not(bent))
            def _(k=k):
                second(me, k, True).start()

        for h in range(2):
            local(h).start()
        cnt[...] = jnp.full(cnt.shape, count[0], jnp.int32)
        count_first().start()

        @pl.when(jnp.logical_not(bent))
        def _():
            count_second().start()

        full[...] = jnp.zeros_like(full)
        fsum[...] = jnp.zeros_like(fsum)
        gsum[...] = jnp.zeros_like(gsum)
        for h in range(2):
            local(h).wait()
        for k in range(3):
            own_part(me, g, k, True)
        for k in range(3):
            zr_wait(fd, o, k)
            along(fd, o, k, False, ot).start()
            zr_wait(ot, g, k)
            across(ot, k, False)
            turn(me, k)
            own_part(me, o, k, True)
            if k == 2:
                along(me, g, 0, True, ot).start()

        @pl.when(bends)
        def _():
            cr_wait(2)
            count_bend().start()

        for k in range(1, 3):
            along(me, g, k, True, ot).start()
        gt[...] = jnp.zeros_like(gt)
        for k in range(3):
            pass_on(me, k)
        cr_wait(1)
        count_relay().start()
        for k in range(3):
            own_part(ot, g, k, False)
        for k in range(3):
            zr_wait(fd, g, k)
            along(fd, g, k, False, ot).start()
            first(fd, k, False).start()
            zr_wait(of, g, k)
            across(of, k, False)
            turn(ot, k)
            own_part(fd, o, k, False)
            if k == 0:
                settle(me, True)
                partner_part(me, True)
                multiply(me, g, True)
            if k == 1:
                multiply(me, o, True)
        for k in range(3):
            pass_on(ot, k)
        for k in range(3):
            own_part(fd, g, k, False)
        settle(ot, True)
        partner_part(ot, False)
        multiply(ot, g)
        for k in range(3):
            turn(of, k)
            own_part(of, g, k, False)
        for k in range(3):
            zr_wait(ot, o, k)
            own_part(ot, o, k, False)
            multiply_rows(ot, o, k)
        for k in range(3):
            pass_on(fd, k)
        for k in range(3):
            pass_on(of, k)
        settle(fd, False)
        partner_part(fd, False)
        multiply(fd, g)
        multiply(fd, o)
        settle(of, True)
        partner_part(of, False)
        multiply(of, g)
        cr_wait(0)

        @pl.when(jnp.logical_not(bends))
        def _():
            cr_wait(2)

        tile(g)
        for k in range(3):
            zr_wait(of, o, k)
            own_part(of, o, k, False)
            multiply_rows(of, o, k)
        tile(o)
        finish()

    def finish():
        for k in range(3):
            for h in range(2):
                along(me, h, k, True, ot).wait_send()
                along(fd, h, k, False, ot).wait_send()
            for s in (me, ot, of):
                first(s, k, False).wait_send()
                relay(s, k).wait_send()

                @pl.when(jnp.logical_not(bent))
                def _(s=s, k=k):
                    second(s, k, False).wait_send()

                @pl.when(bends)
                def _(s=s, k=k):
                    bend(s, k).wait_send()

            relay(fd, k).wait_send()
            first(fd, k, False).wait_send()

        count_first().wait_send()
        count_relay().wait_send()

        @pl.when(jnp.logical_not(bent))
        def _():
            count_second().wait_send()

        @pl.when(bends)
        def _():
            count_bend().wait_send()

        for d in range(ROUNDS):
            for h in range(2):
                for j in range(2):
                    ahead_copy(h, d, j).wait_send()

                    @pl.when(2 * h + j != z)
                    def _(h=h, d=d, j=j):
                        behind_copy(h, d, j).wait_send()

                ahead_wait(d, h)
            behind_wait(d, o)

    @pl.when(inner == 0)
    def _():
        feeder()

    @pl.when(inner == 1)
    def _():
        worker()


def shards(n, reps, coords, frame_count):
    atoms, frames = coords.shape[1], coords.shape[2]
    half = frames // 2
    pitch = (atoms + 15) // 16 * 16
    again = (2 * pitch + 127) // 128 * 128
    depth = again + (pitch + 127) // 128 * 128
    f32, bf16 = jnp.float32, jnp.bfloat16
    dma = pltpu.SemaphoreType.DMA
    vmem = pl.BlockSpec(memory_space=pltpu.VMEM)
    result = jax.ShapeDtypeStruct((ROUNDS, frames // reps, frames), f32)
    return pl.pallas_call(
        functools.partial(kernel, n, reps),
        out_shape=(result, result),
        in_specs=[pl.BlockSpec(memory_space=pl.ANY), pl.BlockSpec(memory_space=pltpu.SMEM)],
        out_specs=(vmem, vmem),
        scratch_shapes=[
            pltpu.VMEM((reps, 2, 3, atoms, half), f32),
            pltpu.VMEM((ROUNDS, reps, 3, atoms, half), f32),
            pltpu.VMEM((8, half), jnp.int32),
            pltpu.VMEM((ROUNDS, 8, half), jnp.int32),
            pltpu.VMEM((again, half), f32),
            pltpu.VMEM((2, reps, 3 * half, depth), bf16),
            pltpu.VMEM((reps, depth, ROUNDS * 3 * half), bf16),
            pltpu.VMEM((2, 3 * half, ROUNDS * 3 * half), f32),
            pltpu.VMEM((2, 3, 8, half), f32),
            pltpu.VMEM((2, 4, 8, half), f32),
            pltpu.VMEM((ROUNDS, 3, 8, half), f32),
            pltpu.VMEM((ROUNDS, 4, 8, half), f32),
            pltpu.VMEM((4, half, half), f32),
            pltpu.VMEM((2, ROUNDS, half, half), f32),
            pltpu.VMEM((2, ROUNDS, half, half), f32),
            dma((2, 2, 3)),
            dma((reps, 2, 3)),
            dma((3,)),
            dma((4, reps, 3)),
            dma((ROUNDS, reps, 3)),
            dma((4,)),
            dma((ROUNDS,)),
            dma((2, ROUNDS, 4)),
            dma((ROUNDS, 2)),
            dma((ROUNDS, 2)),
            dma((2,)),
            pltpu.SemaphoreType.REGULAR,
        ],
        compiler_params=pltpu.CompilerParams(collective_id=0, has_side_effects=True,
                                             vmem_limit_bytes=53 * 1024 * 1024),
    )(coords, frame_count.astype(jnp.int32))


def solution(mesh):
    in_specs = (P(None, "rep", "blk"), P("blk"))
    out_specs = (P(None, ("blk", "rep"), None), P(None, ("blk", "rep"), None))
    body = functools.partial(shards, mesh.shape["blk"], mesh.shape["rep"])
    return jax.shard_map(body, mesh=mesh, in_specs=in_specs, out_specs=out_specs, check_vma=False)
```

```python
import functools

import jax
import jax.numpy as jnp
from jax import lax
from jax.experimental import pallas as pl
from jax.experimental.pallas import tpu as pltpu
from jax.sharding import PartitionSpec as P

ROUNDS = 3
NEWTON = 4
MESH = pl.DeviceIdType.MESH


def pair_minor(upper, lower, left, right):
    return upper[left] * lower[right] - upper[right] * lower[left]


def deviation(m, total):
    keyed = [
        [m[0][0] + m[1][1] + m[2][2], m[1][2] - m[2][1], m[2][0] - m[0][2], m[0][1] - m[1][0]],
        [m[1][2] - m[2][1], m[0][0] - m[1][1] - m[2][2], m[0][1] + m[1][0], m[2][0] + m[0][2]],
        [m[2][0] - m[0][2], m[0][1] + m[1][0], -m[0][0] + m[1][1] - m[2][2], m[1][2] + m[2][1]],
        [m[0][1] - m[1][0], m[2][0] + m[0][2], m[1][2] + m[2][1], -m[0][0] - m[1][1] + m[2][2]],
    ]
    top_one, top_two, low_one, low_two = keyed
    det_key = (
        pair_minor(top_one, top_two, 0, 1) * pair_minor(low_one, low_two, 2, 3)
        - pair_minor(top_one, top_two, 0, 2) * pair_minor(low_one, low_two, 1, 3)
        + pair_minor(top_one, top_two, 0, 3) * pair_minor(low_one, low_two, 1, 2)
        + pair_minor(top_one, top_two, 1, 2) * pair_minor(low_one, low_two, 0, 3)
        - pair_minor(top_one, top_two, 1, 3) * pair_minor(low_one, low_two, 0, 2)
        + pair_minor(top_one, top_two, 2, 3) * pair_minor(low_one, low_two, 0, 1)
    )
    det_three = (
        m[0][0] * (m[1][1] * m[2][2] - m[1][2] * m[2][1])
        - m[0][1] * (m[1][0] * m[2][2] - m[1][2] * m[2][0])
        + m[0][2] * (m[1][0] * m[2][1] - m[1][1] * m[2][0])
    )
    square_sum = m[0][0] * m[0][0]
    for first in range(3):
        for second in range(3):
            if first + second > 0:
                square_sum = square_sum + m[first][second] * m[first][second]
    second_coef = -2.0 * square_sum
    first_coef = -8.0 * det_three
    largest = 0.5 * total
    for newton_step in range(NEWTON):
        squared = largest * largest
        polynomial = squared * squared + second_coef * squared + first_coef * largest + det_key
        derivative = 4.0 * squared * largest + 2.0 * second_coef * largest + first_coef
        largest = largest - polynomial / derivative
    return total - 2.0 * largest


def split(value):
    high = value.astype(jnp.bfloat16)
    low = (value - high.astype(jnp.float32)).astype(jnp.bfloat16)
    return high, low


def kernel(n, reps, coords, count, both, own, part, cnt, pcnt, full, ft, gt, cov,
           fshift, fsum, gshift, gsum, col, dev, devt,
           zs, zr, fs, xs, pr, cs, cr, os, br, ar, ls, go):
    behind, ahead = both.at[0], both.at[1]
    b = lax.axis_index("blk")
    z = lax.axis_index("rep")
    par = lax.rem(b, 2)
    odd = lax.rem(b // 2, 2)
    bent = odd * par == 1
    bends = odd * (1 - par) == 1
    atoms = coords.shape[1]
    half = coords.shape[2] // 2
    quarter = half // 2
    natom = atoms * reps
    pitch = (atoms + 15) // 16 * 16
    again = full.shape[0]
    tail = ft.shape[3] - again
    g = z // 2
    o = 1 - g
    me = z
    fd = (reps - 1) * g
    of = reps - 1 - fd
    ot = reps - 1 - z
    wk = 1 + g
    inner = jnp.minimum(z, 1) * jnp.minimum(reps - 1 - z, 1)

    def at(step):
        return lax.rem(b + step + n, n)

    barrier = pltpu.get_barrier_semaphore()
    pl.semaphore_signal(barrier, inc=1, device_id=(at(1 - 2 * par), z), device_id_type=MESH)

    @pl.when(odd == 1)
    def _():
        pl.semaphore_signal(barrier, inc=1, device_id=(at(-2), z), device_id_type=MESH)

    @pl.when(par == 0)
    def _():
        pl.semaphore_signal(barrier, inc=1, device_id=(at(-3), z), device_id_type=MESH)

    @pl.when(odd + par == 1)
    def _():
        pl.semaphore_signal(barrier, inc=1, device_id=(at(1 - 2 * odd), z), device_id_type=MESH)

    @pl.when(inner == 1)
    def _():
        for where in (ot, fd):
            pl.semaphore_signal(barrier, inc=1, device_id=(b, where), device_id_type=MESH)

    pl.semaphore_wait(barrier, 3 + 2 * (1 - odd) * par)

    @pl.when((odd == 0) & (par == 1))
    def _():
        pl.semaphore_signal(go, inc=1, device_id=(at(1), z), device_id_type=MESH)

    def remote(src, dst, send, recv, where):
        return pltpu.make_async_remote_copy(src_ref=src, dst_ref=dst, send_sem=send, recv_sem=recv,
                                            device_id=where, device_id_type=MESH)

    def lanes(h):
        return pl.ds(pl.multiple_of(h * half, half), half)

    def source(s, h, k, mine):
        return coords.at[k, :, lanes(h)] if mine else own.at[s, h, k]

    def along(s, h, k, mine, where):
        return remote(source(s, h, k, mine), own.at[s, h, k], zs.at[1 - mine, h, k], zr.at[s, h, k],
                      (b, where))

    def first(s, k, mine):
        slot = 2 * par
        return remote(source(s, g, k, mine), part.at[slot, s, k], xs.at[1, s, k], pr.at[slot, s, k],
                      (at(1 + slot), z))

    def second(s, k, mine):
        return remote(source(s, g, k, mine), part.at[1, s, k], xs.at[0, s, k], pr.at[1, s, k],
                      (at(2), z))

    def bend(s, k):
        return remote(part.at[2, s, k], part.at[1, s, k], xs.at[3, s, k], pr.at[1, s, k],
                      (at(-1), z))

    def relay(s, k):
        slot = 2 - 2 * par
        return remote(part.at[1, s, k], part.at[slot, s, k], xs.at[2, s, k], pr.at[slot, s, k],
                      (at(1 - 2 * par), z))

    def feed(k):
        return remote(part.at[1, z, k], part.at[1, z, k], fs.at[k], pr.at[1, z, k], (b, wk))

    def count_first():
        slot = 2 * par
        return remote(cnt, pcnt.at[slot], cs.at[1], cr.at[slot], (at(1 + slot), z))

    def count_second():
        return remote(cnt, pcnt.at[1], cs.at[0], cr.at[1], (at(2), z))

    def count_bend():
        return remote(pcnt.at[2], pcnt.at[1], cs.at[3], cr.at[1], (at(-1), z))

    def count_relay():
        slot = 2 - 2 * par
        return remote(pcnt.at[1], pcnt.at[slot], cs.at[2], cr.at[slot], (at(1 - 2 * par), z))

    def zr_wait(s, h, k):
        remote(own.at[s, h, k], own.at[s, h, k], zs.at[0, h, k], zr.at[s, h, k],
               (b, lax.rem(z + 1, reps))).wait_recv()

    def pr_wait(d, s, k):
        remote(part.at[d, s, k], part.at[d, s, k], xs.at[0, s, k], pr.at[d, s, k],
               (b, lax.rem(z + 1, reps))).wait_recv()

    def cr_wait(d):
        remote(pcnt.at[d], pcnt.at[d], cs.at[0], cr.at[d], (b, lax.rem(z + 1, reps))).wait_recv()

    def local(h):
        return pltpu.make_async_copy(coords.at[:, :, lanes(h)], own.at[z, h], ls.at[h])

    def behind_copy(h, d, j):
        return remote(dev.at[h, d, pl.ds(j * quarter, quarter)], behind.at[d, :, lanes(g)],
                      os.at[h, d, 2 + j], br.at[d, g], (b, 2 * h + j))

    def ahead_copy(h, d, j):
        return remote(devt.at[h, d, pl.ds(j * quarter, quarter)], ahead.at[d, :, lanes(h)],
                      os.at[h, d, j], ar.at[d, h], (lax.rem(b - 1 - d + n, n), 2 * g + j))

    def ahead_wait(d, h):
        remote(devt.at[0, d, pl.ds(0, quarter)], ahead.at[d, :, pl.ds(h * half, half)],
               os.at[0, d, 0], ar.at[d, h], (at(1), z)).wait_recv()

    def behind_wait(d, side):
        remote(dev.at[0, d, pl.ds(0, quarter)], behind.at[d, :, lanes(side)],
               os.at[0, d, 2], br.at[d, side], (at(1), z)).wait_recv()

    def feeder():
        for k in range(3):
            along(me, o, k, True, wk).start()

            @pl.when(bent)
            def _(k=k):
                first(me, k, True).start()

        @pl.when(bends)
        def _():
            pl.semaphore_wait(go, 1)

        for k in range(3):
            @pl.when(jnp.logical_not(bent))
            def _(k=k):
                second(me, k, True).start()

        for k in range(3):
            along(me, g, k, True, wk).start()
        for k in range(3):
            turn(me, k)
        for k in range(3):
            pr_wait(1, me, k)
            feed(k).start()
        for k in range(3):
            along(me, o, k, True, wk).wait_send()
            along(me, g, k, True, wk).wait_send()
            feed(k).wait_send()

            @pl.when(bent)
            def _(k=k):
                first(me, k, True).wait_send()

            @pl.when(jnp.logical_not(bent))
            def _(k=k):
                second(me, k, True).wait_send()

            @pl.when(bends)
            def _(k=k):
                bend(me, k).wait_send()

        for d in range(ROUNDS):
            for side in range(2):
                behind_wait(d, side)
                ahead_wait(d, side)

    def across(s, k, mine):
        first(s, k, mine).start()

        @pl.when(jnp.logical_not(bent))
        def _():
            second(s, k, mine).start()

    def turn(s, k):
        @pl.when(bends)
        def _():
            pr_wait(2, s, k)
            bend(s, k).start()

    def pass_on(s, k):
        pr_wait(1, s, k)
        relay(s, k).start()

    def settle(s, bent_in):
        for k in range(3):
            pr_wait(0, s, k)

            if bent_in:
                @pl.when(jnp.logical_not(bends))
                def _(k=k):
                    pr_wait(2, s, k)
            else:
                pr_wait(2, s, k)

    def own_part(s, h, k, start):
        value = own[s, h, k]
        if start:
            shift = jnp.sum(value, axis=0, keepdims=True) / atoms
            fshift[h, k, 0:1, :] = shift
        else:
            shift = fshift[h, k, 0:1, :]
        value = value - shift
        total = jnp.sum(value, axis=0, keepdims=True)
        square = jnp.sum(value * value, axis=0, keepdims=True)
        fsum[h, k, 0:1, :] = fsum[h, k, 0:1, :] + total
        fsum[h, 3, 0:1, :] = fsum[h, 3, 0:1, :] + square
        high = value.astype(jnp.bfloat16).astype(jnp.float32)
        full[0:atoms, :] = high
        full[pitch:pitch + atoms, :] = value - high
        turned = full[...].T.astype(jnp.bfloat16)
        ft[h, s, k * half:(k + 1) * half, 0:again] = turned
        ft[h, s, k * half:(k + 1) * half, again:again + tail] = turned[:, 0:tail]

    def partner_part(s, start):
        for d in range(ROUNDS):
            for k in range(3):
                value = part[d, s, k]
                if start:
                    shift = jnp.sum(value, axis=0, keepdims=True) / atoms
                    gshift[d, k, 0:1, :] = shift
                else:
                    shift = gshift[d, k, 0:1, :]
                value = value - shift
                total = jnp.sum(value, axis=0, keepdims=True)
                square = jnp.sum(value * value, axis=0, keepdims=True)
                gsum[d, k, 0:1, :] = gsum[d, k, 0:1, :] + total
                gsum[d, 3, 0:1, :] = gsum[d, 3, 0:1, :] + square
                high, low = split(value)
                place = slice((3 * d + k) * half, (3 * d + k + 1) * half)
                gt[s, 0:atoms, place] = high
                gt[s, pitch:pitch + atoms, place] = high
                gt[s, again:again + atoms, place] = low

    product = functools.partial(jnp.dot, preferred_element_type=jnp.float32)

    def multiply(s, h, start=False):
        term = product(ft[h, s], gt[s])
        cov[h] = term if start else cov[h] + term

    def multiply_rows(s, h, k):
        rows = slice(k * half, (k + 1) * half)
        cov[h, rows, :] = cov[h, rows, :] + product(ft[h, s, rows, :], gt[s])

    def tile(h):
        square = fsum[h, 3, 0:1, :] / natom
        for k in range(3):
            mean = fsum[h, k, 0:1, :] / natom
            square = square - mean * mean
            col[k] = jnp.broadcast_to(mean, (half, half)).T
        col[3] = jnp.broadcast_to(square, (half, half)).T
        rows = half // 4

        def block(d, carry):
            mean = [gsum[d, k, 0:1, :] / natom for k in range(3)]
            other_square = gsum[d, 3, 0:1, :] / natom
            for k in range(3):
                other_square = other_square - mean[k] * mean[k]

            def chunk(i, inner_carry):
                r = pl.multiple_of(i * rows, rows)
                m = [[cov[h, pl.ds(k * half + r, rows), lanes(3 * d + l)] * (1.0 / natom)
                      - col[k, pl.ds(r, rows), :] * mean[l] for l in range(3)] for k in range(3)]
                total = col[3, pl.ds(r, rows), :] + other_square
                frame = h * half + r + lax.broadcasted_iota(jnp.int32, (rows, half), 0)
                other = g * half + lax.broadcasted_iota(jnp.int32, (rows, half), 1)
                mask = (frame < cnt[0:1, :]) & (other < pcnt[d, 0:1, :])
                dev[h, d, pl.ds(r, rows), :] = jnp.where(mask, deviation(m, total), 0.0)
                return inner_carry

            lax.fori_loop(0, half // rows, chunk, 0, unroll=True)
            for j in range(2):
                @pl.when(2 * h + j != z)
                def _(j=j):
                    behind_copy(h, d, j).start()

                @pl.when(2 * h + j == z)
                def _(j=j):
                    behind[d, :, lanes(g)] = dev[h, d, j * quarter:(j + 1) * quarter, :]

            devt[h, d] = dev[h, d].T
            for j in range(2):
                ahead_copy(h, d, j).start()
            return carry

        lax.fori_loop(0, ROUNDS, block, 0)

    def worker():
        for k in range(3):
            along(me, o, k, True, ot).start()
            first(me, k, True).start()

        @pl.when(bends)
        def _():
            pl.semaphore_wait(go, 1)

        for k in range(3):
            @pl.when(jnp.logical_not(bent))
            def _(k=k):
                second(me, k, True).start()

        for h in range(2):
            local(h).start()
        cnt[...] = jnp.full(cnt.shape, count[0], jnp.int32)
        count_first().start()

        @pl.when(jnp.logical_not(bent))
        def _():
            count_second().start()

        full[...] = jnp.zeros_like(full)
        fsum[...] = jnp.zeros_like(fsum)
        gsum[...] = jnp.zeros_like(gsum)
        for h in range(2):
            local(h).wait()
        for k in range(3):
            own_part(me, g, k, True)
        for k in range(3):
            zr_wait(fd, o, k)
            along(fd, o, k, False, ot).start()
            zr_wait(ot, g, k)
            across(ot, k, False)
            turn(me, k)
            own_part(me, o, k, True)
            if k == 2:
                along(me, g, 0, True, ot).start()

        @pl.when(bends)
        def _():
            cr_wait(2)
            count_bend().start()

        for k in range(1, 3):
            along(me, g, k, True, ot).start()
        gt[...] = jnp.zeros_like(gt)
        for k in range(3):
            pass_on(me, k)
        cr_wait(1)
        count_relay().start()
        for k in range(3):
            own_part(ot, g, k, False)
        for k in range(3):
            zr_wait(fd, g, k)
            along(fd, g, k, False, ot).start()
            first(fd, k, False).start()
            zr_wait(of, g, k)
            across(of, k, False)
            turn(ot, k)
            own_part(fd, o, k, False)
            if k == 0:
                settle(me, True)
                partner_part(me, True)
                multiply(me, g, True)
            if k == 1:
                multiply(me, o, True)
        for k in range(3):
            pass_on(ot, k)
        for k in range(3):
            own_part(fd, g, k, False)
        settle(ot, True)
        partner_part(ot, False)
        multiply(ot, g)
        for k in range(3):
            turn(of, k)
            own_part(of, g, k, False)
        for k in range(3):
            zr_wait(ot, o, k)
            own_part(ot, o, k, False)
            multiply_rows(ot, o, k)
        for k in range(3):
            pass_on(fd, k)
        for k in range(3):
            pass_on(of, k)
        settle(fd, False)
        partner_part(fd, False)
        multiply(fd, g)
        multiply(fd, o)
        settle(of, True)
        partner_part(of, False)
        multiply(of, g)
        cr_wait(0)

        @pl.when(jnp.logical_not(bends))
        def _():
            cr_wait(2)

        tile(g)
        for k in range(3):
            zr_wait(of, o, k)
            own_part(of, o, k, False)
            multiply_rows(of, o, k)
        tile(o)
        finish()

    def finish():
        for k in range(3):
            for h in range(2):
                along(me, h, k, True, ot).wait_send()
                along(fd, h, k, False, ot).wait_send()
            for s in (me, ot, of):
                first(s, k, False).wait_send()
                relay(s, k).wait_send()

                @pl.when(jnp.logical_not(bent))
                def _(s=s, k=k):
                    second(s, k, False).wait_send()

                @pl.when(bends)
                def _(s=s, k=k):
                    bend(s, k).wait_send()

            relay(fd, k).wait_send()
            first(fd, k, False).wait_send()

        count_first().wait_send()
        count_relay().wait_send()

        @pl.when(jnp.logical_not(bent))
        def _():
            count_second().wait_send()

        @pl.when(bends)
        def _():
            count_bend().wait_send()

        for d in range(ROUNDS):
            for h in range(2):
                for j in range(2):
                    ahead_copy(h, d, j).wait_send()

                    @pl.when(2 * h + j != z)
                    def _(h=h, d=d, j=j):
                        behind_copy(h, d, j).wait_send()

                ahead_wait(d, h)
            behind_wait(d, o)

    @pl.when(inner == 0)
    def _():
        feeder()

    @pl.when(inner == 1)
    def _():
        worker()


def shards(n, reps, coords, frame_count):
    atoms, frames = coords.shape[1], coords.shape[2]
    half = frames // 2
    pitch = (atoms + 15) // 16 * 16
    again = (2 * pitch + 127) // 128 * 128
    depth = again + (pitch + 127) // 128 * 128
    f32, bf16 = jnp.float32, jnp.bfloat16
    dma = pltpu.SemaphoreType.DMA
    vmem = pl.BlockSpec(memory_space=pltpu.VMEM)
    result = jax.ShapeDtypeStruct((2, ROUNDS, frames // reps, frames), f32)
    made = pl.pallas_call(
        functools.partial(kernel, n, reps),
        out_shape=result,
        in_specs=[pl.BlockSpec(memory_space=pl.ANY), pl.BlockSpec(memory_space=pltpu.SMEM)],
        out_specs=vmem,
        scratch_shapes=[
            pltpu.VMEM((reps, 2, 3, atoms, half), f32),
            pltpu.VMEM((ROUNDS, reps, 3, atoms, half), f32),
            pltpu.VMEM((8, half), jnp.int32),
            pltpu.VMEM((ROUNDS, 8, half), jnp.int32),
            pltpu.VMEM((again, half), f32),
            pltpu.VMEM((2, reps, 3 * half, depth), bf16),
            pltpu.VMEM((reps, depth, ROUNDS * 3 * half), bf16),
            pltpu.VMEM((2, 3 * half, ROUNDS * 3 * half), f32),
            pltpu.VMEM((2, 3, 8, half), f32),
            pltpu.VMEM((2, 4, 8, half), f32),
            pltpu.VMEM((ROUNDS, 3, 8, half), f32),
            pltpu.VMEM((ROUNDS, 4, 8, half), f32),
            pltpu.VMEM((4, half, half), f32),
            pltpu.VMEM((2, ROUNDS, half, half), f32),
            pltpu.VMEM((2, ROUNDS, half, half), f32),
            dma((2, 2, 3)),
            dma((reps, 2, 3)),
            dma((3,)),
            dma((4, reps, 3)),
            dma((ROUNDS, reps, 3)),
            dma((4,)),
            dma((ROUNDS,)),
            dma((2, ROUNDS, 4)),
            dma((ROUNDS, 2)),
            dma((ROUNDS, 2)),
            dma((2,)),
            pltpu.SemaphoreType.REGULAR,
        ],
        compiler_params=pltpu.CompilerParams(collective_id=0, has_side_effects=True,
                                             vmem_limit_bytes=53 * 1024 * 1024),
    )(coords, frame_count.astype(jnp.int32))
    return made[0], made[1]


def solution(mesh):
    in_specs = (P(None, "rep", "blk"), P("blk"))
    out_specs = (P(None, ("blk", "rep"), None), P(None, ("blk", "rep"), None))
    body = functools.partial(shards, mesh.shape["blk"], mesh.shape["rep"])
    return jax.shard_map(body, mesh=mesh, in_specs=in_specs, out_specs=out_specs, check_vma=False)
```

```python
import functools

import jax
import jax.numpy as jnp
from jax import lax
from jax.experimental import pallas as pl
from jax.experimental.pallas import tpu as pltpu
from jax.sharding import PartitionSpec as P

ROUNDS = 3
NEWTON = 4
MESH = pl.DeviceIdType.MESH


def pair_minor(upper, lower, left, right):
    return upper[left] * lower[right] - upper[right] * lower[left]


def deviation(m, total):
    keyed = [
        [m[0][0] + m[1][1] + m[2][2], m[1][2] - m[2][1], m[2][0] - m[0][2], m[0][1] - m[1][0]],
        [m[1][2] - m[2][1], m[0][0] - m[1][1] - m[2][2], m[0][1] + m[1][0], m[2][0] + m[0][2]],
        [m[2][0] - m[0][2], m[0][1] + m[1][0], -m[0][0] + m[1][1] - m[2][2], m[1][2] + m[2][1]],
        [m[0][1] - m[1][0], m[2][0] + m[0][2], m[1][2] + m[2][1], -m[0][0] - m[1][1] + m[2][2]],
    ]
    top_one, top_two, low_one, low_two = keyed
    det_key = (
        pair_minor(top_one, top_two, 0, 1) * pair_minor(low_one, low_two, 2, 3)
        - pair_minor(top_one, top_two, 0, 2) * pair_minor(low_one, low_two, 1, 3)
        + pair_minor(top_one, top_two, 0, 3) * pair_minor(low_one, low_two, 1, 2)
        + pair_minor(top_one, top_two, 1, 2) * pair_minor(low_one, low_two, 0, 3)
        - pair_minor(top_one, top_two, 1, 3) * pair_minor(low_one, low_two, 0, 2)
        + pair_minor(top_one, top_two, 2, 3) * pair_minor(low_one, low_two, 0, 1)
    )
    det_three = (
        m[0][0] * (m[1][1] * m[2][2] - m[1][2] * m[2][1])
        - m[0][1] * (m[1][0] * m[2][2] - m[1][2] * m[2][0])
        + m[0][2] * (m[1][0] * m[2][1] - m[1][1] * m[2][0])
    )
    square_sum = m[0][0] * m[0][0]
    for first in range(3):
        for second in range(3):
            if first + second > 0:
                square_sum = square_sum + m[first][second] * m[first][second]
    second_coef = -2.0 * square_sum
    first_coef = -8.0 * det_three
    largest = 0.5 * total
    for newton_step in range(NEWTON):
        squared = largest * largest
        polynomial = squared * squared + second_coef * squared + first_coef * largest + det_key
        derivative = 4.0 * squared * largest + 2.0 * second_coef * largest + first_coef
        largest = largest - polynomial / derivative
    return total - 2.0 * largest


def split(value):
    high = value.astype(jnp.bfloat16)
    low = (value - high.astype(jnp.float32)).astype(jnp.bfloat16)
    return high, low


def kernel(n, reps, coords, count, both, own, part, cnt, pcnt, full, ft, gt, cov,
           fshift, fsum, gshift, gsum, col, dev, devt,
           zs, zr, fs, xs, pr, cs, cr, os, br, ar, ls, go):
    behind, ahead = both.at[0], both.at[1]
    b = lax.axis_index("blk")
    z = lax.axis_index("rep")
    par = lax.rem(b, 2)
    odd = lax.rem(b // 2, 2)
    bent = odd * par == 1
    bends = odd * (1 - par) == 1
    atoms = coords.shape[1]
    half = coords.shape[2] // 2
    quarter = half // 2
    natom = atoms * reps
    pitch = (atoms + 15) // 16 * 16
    again = full.shape[0]
    tail = ft.shape[3] - again
    g = z // 2
    o = 1 - g
    me = z
    fd = (reps - 1) * g
    of = reps - 1 - fd
    ot = reps - 1 - z
    wk = 1 + g
    inner = jnp.minimum(z, 1) * jnp.minimum(reps - 1 - z, 1)

    def at(step):
        return lax.rem(b + step + n, n)

    barrier = pltpu.get_barrier_semaphore()
    pl.semaphore_signal(barrier, inc=1, device_id=(at(1 - 2 * par), z), device_id_type=MESH)

    @pl.when(odd == 1)
    def _():
        pl.semaphore_signal(barrier, inc=1, device_id=(at(-2), z), device_id_type=MESH)

    @pl.when(par == 0)
    def _():
        pl.semaphore_signal(barrier, inc=1, device_id=(at(-3), z), device_id_type=MESH)

    @pl.when(odd + par == 1)
    def _():
        pl.semaphore_signal(barrier, inc=1, device_id=(at(1 - 2 * odd), z), device_id_type=MESH)

    @pl.when(inner == 1)
    def _():
        for where in (ot, fd):
            pl.semaphore_signal(barrier, inc=1, device_id=(b, where), device_id_type=MESH)

    pl.semaphore_wait(barrier, 3 + 2 * (1 - odd) * par)

    @pl.when((odd == 0) & (par == 1))
    def _():
        pl.semaphore_signal(go, inc=1, device_id=(at(1), z), device_id_type=MESH)

    def remote(src, dst, send, recv, where):
        return pltpu.make_async_remote_copy(src_ref=src, dst_ref=dst, send_sem=send, recv_sem=recv,
                                            device_id=where, device_id_type=MESH)

    def lanes(h):
        return pl.ds(pl.multiple_of(h * half, half), half)

    def source(s, h, k, mine):
        return coords.at[k, :, lanes(h)] if mine else own.at[s, h, k]

    def along(s, h, k, mine, where):
        return remote(source(s, h, k, mine), own.at[s, h, k], zs.at[1 - mine, h, k], zr.at[s, h, k],
                      (b, where))

    def first(s, k, mine):
        slot = 2 * par
        return remote(source(s, g, k, mine), part.at[slot, s, k], xs.at[1, s, k], pr.at[slot, s, k],
                      (at(1 + slot), z))

    def second(s, k, mine):
        return remote(source(s, g, k, mine), part.at[1, s, k], xs.at[0, s, k], pr.at[1, s, k],
                      (at(2), z))

    def bend(s, k):
        return remote(part.at[2, s, k], part.at[1, s, k], xs.at[3, s, k], pr.at[1, s, k],
                      (at(-1), z))

    def relay(s, k):
        slot = 2 - 2 * par
        return remote(part.at[1, s, k], part.at[slot, s, k], xs.at[2, s, k], pr.at[slot, s, k],
                      (at(1 - 2 * par), z))

    def feed(k):
        return remote(part.at[1, z, k], part.at[1, z, k], fs.at[k], pr.at[1, z, k], (b, wk))

    def count_first():
        slot = 2 * par
        return remote(cnt, pcnt.at[slot], cs.at[1], cr.at[slot], (at(1 + slot), z))

    def count_second():
        return remote(cnt, pcnt.at[1], cs.at[0], cr.at[1], (at(2), z))

    def count_bend():
        return remote(pcnt.at[2], pcnt.at[1], cs.at[3], cr.at[1], (at(-1), z))

    def count_relay():
        slot = 2 - 2 * par
        return remote(pcnt.at[1], pcnt.at[slot], cs.at[2], cr.at[slot], (at(1 - 2 * par), z))

    def zr_wait(s, h, k):
        remote(own.at[s, h, k], own.at[s, h, k], zs.at[0, h, k], zr.at[s, h, k],
               (b, lax.rem(z + 1, reps))).wait_recv()

    def pr_wait(d, s, k):
        remote(part.at[d, s, k], part.at[d, s, k], xs.at[0, s, k], pr.at[d, s, k],
               (b, lax.rem(z + 1, reps))).wait_recv()

    def cr_wait(d):
        remote(pcnt.at[d], pcnt.at[d], cs.at[0], cr.at[d], (b, lax.rem(z + 1, reps))).wait_recv()

    def local(h):
        return pltpu.make_async_copy(coords.at[:, :, lanes(h)], own.at[z, h], ls.at[h])

    def behind_copy(h, d, j):
        return remote(dev.at[h, d, pl.ds(j * quarter, quarter)], behind.at[d, :, lanes(g)],
                      os.at[h, d, 2 + j], br.at[d, g], (b, 2 * h + j))

    def ahead_copy(h, d, j):
        return remote(devt.at[h, d, pl.ds(j * quarter, quarter)], ahead.at[d, :, lanes(h)],
                      os.at[h, d, j], ar.at[d, h], (lax.rem(b - 1 - d + n, n), 2 * g + j))

    def ahead_wait(d, h):
        remote(devt.at[0, d, pl.ds(0, quarter)], ahead.at[d, :, pl.ds(h * half, half)],
               os.at[0, d, 0], ar.at[d, h], (at(1), z)).wait_recv()

    def behind_wait(d, side):
        remote(dev.at[0, d, pl.ds(0, quarter)], behind.at[d, :, lanes(side)],
               os.at[0, d, 2], br.at[d, side], (at(1), z)).wait_recv()

    def feeder():
        for k in range(3):
            along(me, o, k, True, wk).start()

            @pl.when(bent)
            def _(k=k):
                first(me, k, True).start()

        @pl.when(bends)
        def _():
            pl.semaphore_wait(go, 1)

        for k in range(3):
            @pl.when(jnp.logical_not(bent))
            def _(k=k):
                second(me, k, True).start()

        for k in range(3):
            along(me, g, k, True, wk).start()
        for k in range(3):
            turn(me, k)
        for k in range(3):
            pr_wait(1, me, k)
            feed(k).start()
        for k in range(3):
            along(me, o, k, True, wk).wait_send()
            along(me, g, k, True, wk).wait_send()
            feed(k).wait_send()

            @pl.when(bent)
            def _(k=k):
                first(me, k, True).wait_send()

            @pl.when(jnp.logical_not(bent))
            def _(k=k):
                second(me, k, True).wait_send()

            @pl.when(bends)
            def _(k=k):
                bend(me, k).wait_send()

        for d in range(ROUNDS):
            for side in range(2):
                behind_wait(d, side)
                ahead_wait(d, side)

    def across(s, k, mine):
        first(s, k, mine).start()

        @pl.when(jnp.logical_not(bent))
        def _():
            second(s, k, mine).start()

    def turn(s, k):
        @pl.when(bends)
        def _():
            pr_wait(2, s, k)
            bend(s, k).start()

    def pass_on(s, k):
        pr_wait(1, s, k)
        relay(s, k).start()

    def settle(s, bent_in):
        for k in range(3):
            pr_wait(0, s, k)

            if bent_in:
                @pl.when(jnp.logical_not(bends))
                def _(k=k):
                    pr_wait(2, s, k)
            else:
                pr_wait(2, s, k)

    def own_part(s, h, k, start):
        value = own[s, h, k]
        if start:
            shift = jnp.sum(value, axis=0, keepdims=True) / atoms
            fshift[h, k, 0:1, :] = shift
        else:
            shift = fshift[h, k, 0:1, :]
        value = value - shift
        total = jnp.sum(value, axis=0, keepdims=True)
        square = jnp.sum(value * value, axis=0, keepdims=True)
        fsum[h, k, 0:1, :] = fsum[h, k, 0:1, :] + total
        fsum[h, 3, 0:1, :] = fsum[h, 3, 0:1, :] + square
        high = value.astype(jnp.bfloat16).astype(jnp.float32)
        full[0:atoms, :] = high
        full[pitch:pitch + atoms, :] = value - high
        turned = full[...].T.astype(jnp.bfloat16)
        ft[h, s, k * half:(k + 1) * half, 0:again] = turned
        ft[h, s, k * half:(k + 1) * half, again:again + tail] = turned[:, 0:tail]

    def partner_part(s, start):
        for d in range(ROUNDS):
            for k in range(3):
                value = part[d, s, k]
                if start:
                    shift = jnp.sum(value, axis=0, keepdims=True) / atoms
                    gshift[d, k, 0:1, :] = shift
                else:
                    shift = gshift[d, k, 0:1, :]
                value = value - shift
                total = jnp.sum(value, axis=0, keepdims=True)
                square = jnp.sum(value * value, axis=0, keepdims=True)
                gsum[d, k, 0:1, :] = gsum[d, k, 0:1, :] + total
                gsum[d, 3, 0:1, :] = gsum[d, 3, 0:1, :] + square
                high, low = split(value)
                place = slice((3 * d + k) * half, (3 * d + k + 1) * half)
                gt[s, 0:atoms, place] = high
                gt[s, pitch:pitch + atoms, place] = high
                gt[s, again:again + atoms, place] = low

    product = functools.partial(jnp.dot, preferred_element_type=jnp.float32)

    def multiply(s, h, start=False):
        term = product(ft[h, s], gt[s])
        cov[h] = term if start else cov[h] + term

    def multiply_rows(s, h, k):
        rows = slice(k * half, (k + 1) * half)
        cov[h, rows, :] = cov[h, rows, :] + product(ft[h, s, rows, :], gt[s])

    def tile(h):
        square = fsum[h, 3, 0:1, :] / natom
        for k in range(3):
            mean = fsum[h, k, 0:1, :] / natom
            square = square - mean * mean
            col[k] = jnp.broadcast_to(mean, (half, half)).T
        col[3] = jnp.broadcast_to(square, (half, half)).T
        rows = half // 4

        def block(d, carry):
            mean = [gsum[d, k, 0:1, :] / natom for k in range(3)]
            other_square = gsum[d, 3, 0:1, :] / natom
            for k in range(3):
                other_square = other_square - mean[k] * mean[k]

            def chunk(i, inner_carry):
                r = pl.multiple_of(i * rows, rows)
                m = [[cov[h, pl.ds(k * half + r, rows), lanes(3 * d + l)] * (1.0 / natom)
                      - col[k, pl.ds(r, rows), :] * mean[l] for l in range(3)] for k in range(3)]
                total = col[3, pl.ds(r, rows), :] + other_square
                frame = h * half + r + lax.broadcasted_iota(jnp.int32, (rows, half), 0)
                other = g * half + lax.broadcasted_iota(jnp.int32, (rows, half), 1)
                mask = (frame < cnt[0:1, :]) & (other < pcnt[d, 0:1, :])
                dev[h, d, pl.ds(r, rows), :] = jnp.where(mask, deviation(m, total), 0.0)
                return inner_carry

            lax.fori_loop(0, half // rows, chunk, 0, unroll=True)
            for j in range(2):
                @pl.when(2 * h + j != z)
                def _(j=j):
                    behind_copy(h, d, j).start()

                @pl.when(2 * h + j == z)
                def _(j=j):
                    behind[d, :, lanes(g)] = dev[h, d, j * quarter:(j + 1) * quarter, :]

            devt[h, d] = dev[h, d].T
            for j in range(2):
                ahead_copy(h, d, j).start()
            return carry

        lax.fori_loop(0, ROUNDS, lambda i, c: block(lax.rem(i + 1, ROUNDS), c), 0)

    def worker():
        for k in range(3):
            along(me, o, k, True, ot).start()
            first(me, k, True).start()

        @pl.when(bends)
        def _():
            pl.semaphore_wait(go, 1)

        for k in range(3):
            @pl.when(jnp.logical_not(bent))
            def _(k=k):
                second(me, k, True).start()

        for h in range(2):
            local(h).start()
        cnt[...] = jnp.full(cnt.shape, count[0], jnp.int32)
        count_first().start()

        @pl.when(jnp.logical_not(bent))
        def _():
            count_second().start()

        full[...] = jnp.zeros_like(full)
        fsum[...] = jnp.zeros_like(fsum)
        gsum[...] = jnp.zeros_like(gsum)
        for h in range(2):
            local(h).wait()
        for k in range(3):
            own_part(me, g, k, True)
        for k in range(3):
            zr_wait(fd, o, k)
            along(fd, o, k, False, ot).start()
            zr_wait(ot, g, k)
            across(ot, k, False)
            turn(me, k)
            own_part(me, o, k, True)
            if k == 2:
                along(me, g, 0, True, ot).start()

        @pl.when(bends)
        def _():
            cr_wait(2)
            count_bend().start()

        for k in range(1, 3):
            along(me, g, k, True, ot).start()
        gt[...] = jnp.zeros_like(gt)
        for k in range(3):
            pass_on(me, k)
        cr_wait(1)
        count_relay().start()
        for k in range(3):
            own_part(ot, g, k, False)
        for k in range(3):
            zr_wait(fd, g, k)
            along(fd, g, k, False, ot).start()
            first(fd, k, False).start()
            zr_wait(of, g, k)
            across(of, k, False)
            turn(ot, k)
            own_part(fd, o, k, False)
            if k == 0:
                settle(me, True)
                partner_part(me, True)
                multiply(me, g, True)
            if k == 1:
                multiply(me, o, True)
        for k in range(3):
            pass_on(ot, k)
        for k in range(3):
            own_part(fd, g, k, False)
        settle(ot, True)
        partner_part(ot, False)
        multiply(ot, g)
        for k in range(3):
            turn(of, k)
            own_part(of, g, k, False)
        for k in range(3):
            zr_wait(ot, o, k)
            own_part(ot, o, k, False)
            multiply_rows(ot, o, k)
        for k in range(3):
            pass_on(fd, k)
        for k in range(3):
            pass_on(of, k)
        settle(fd, False)
        partner_part(fd, False)
        multiply(fd, g)
        multiply(fd, o)
        settle(of, True)
        partner_part(of, False)
        multiply(of, g)
        cr_wait(0)

        @pl.when(jnp.logical_not(bends))
        def _():
            cr_wait(2)

        tile(g)
        for k in range(3):
            zr_wait(of, o, k)
            own_part(of, o, k, False)
            multiply_rows(of, o, k)
        tile(o)
        finish()

    def finish():
        for k in range(3):
            for h in range(2):
                along(me, h, k, True, ot).wait_send()
                along(fd, h, k, False, ot).wait_send()
            for s in (me, ot, of):
                first(s, k, False).wait_send()
                relay(s, k).wait_send()

                @pl.when(jnp.logical_not(bent))
                def _(s=s, k=k):
                    second(s, k, False).wait_send()

                @pl.when(bends)
                def _(s=s, k=k):
                    bend(s, k).wait_send()

            relay(fd, k).wait_send()
            first(fd, k, False).wait_send()

        count_first().wait_send()
        count_relay().wait_send()

        @pl.when(jnp.logical_not(bent))
        def _():
            count_second().wait_send()

        @pl.when(bends)
        def _():
            count_bend().wait_send()

        for d in range(ROUNDS):
            for h in range(2):
                for j in range(2):
                    ahead_copy(h, d, j).wait_send()

                    @pl.when(2 * h + j != z)
                    def _(h=h, d=d, j=j):
                        behind_copy(h, d, j).wait_send()

                ahead_wait(d, h)
            behind_wait(d, o)

    @pl.when(inner == 0)
    def _():
        feeder()

    @pl.when(inner == 1)
    def _():
        worker()


def shards(n, reps, coords, frame_count):
    atoms, frames = coords.shape[1], coords.shape[2]
    half = frames // 2
    pitch = (atoms + 15) // 16 * 16
    again = (2 * pitch + 127) // 128 * 128
    depth = again + (pitch + 127) // 128 * 128
    f32, bf16 = jnp.float32, jnp.bfloat16
    dma = pltpu.SemaphoreType.DMA
    vmem = pl.BlockSpec(memory_space=pltpu.VMEM)
    result = jax.ShapeDtypeStruct((2, ROUNDS, frames // reps, frames), f32)
    made = pl.pallas_call(
        functools.partial(kernel, n, reps),
        out_shape=result,
        in_specs=[pl.BlockSpec(memory_space=pl.ANY), pl.BlockSpec(memory_space=pltpu.SMEM)],
        out_specs=vmem,
        scratch_shapes=[
            pltpu.VMEM((reps, 2, 3, atoms, half), f32),
            pltpu.VMEM((ROUNDS, reps, 3, atoms, half), f32),
            pltpu.VMEM((8, half), jnp.int32),
            pltpu.VMEM((ROUNDS, 8, half), jnp.int32),
            pltpu.VMEM((again, half), f32),
            pltpu.VMEM((2, reps, 3 * half, depth), bf16),
            pltpu.VMEM((reps, depth, ROUNDS * 3 * half), bf16),
            pltpu.VMEM((2, 3 * half, ROUNDS * 3 * half), f32),
            pltpu.VMEM((2, 3, 8, half), f32),
            pltpu.VMEM((2, 4, 8, half), f32),
            pltpu.VMEM((ROUNDS, 3, 8, half), f32),
            pltpu.VMEM((ROUNDS, 4, 8, half), f32),
            pltpu.VMEM((4, half, half), f32),
            pltpu.VMEM((2, ROUNDS, half, half), f32),
            pltpu.VMEM((2, ROUNDS, half, half), f32),
            dma((2, 2, 3)),
            dma((reps, 2, 3)),
            dma((3,)),
            dma((4, reps, 3)),
            dma((ROUNDS, reps, 3)),
            dma((4,)),
            dma((ROUNDS,)),
            dma((2, ROUNDS, 4)),
            dma((ROUNDS, 2)),
            dma((ROUNDS, 2)),
            dma((2,)),
            pltpu.SemaphoreType.REGULAR,
        ],
        compiler_params=pltpu.CompilerParams(collective_id=0, has_side_effects=True,
                                             vmem_limit_bytes=53 * 1024 * 1024),
    )(coords, frame_count.astype(jnp.int32))
    return made[0], made[1]


def solution(mesh):
    in_specs = (P(None, "rep", "blk"), P("blk"))
    out_specs = (P(None, ("blk", "rep"), None), P(None, ("blk", "rep"), None))
    body = functools.partial(shards, mesh.shape["blk"], mesh.shape["rep"])
    return jax.shard_map(body, mesh=mesh, in_specs=in_specs, out_specs=out_specs, check_vma=False)
```

```python
import functools

import jax
import jax.numpy as jnp
from jax import lax
from jax.experimental import pallas as pl
from jax.experimental.pallas import tpu as pltpu
from jax.sharding import PartitionSpec as P

ROUNDS = 3
NEWTON = 4
MESH = pl.DeviceIdType.MESH


def pair_minor(upper, lower, left, right):
    return upper[left] * lower[right] - upper[right] * lower[left]


def deviation(m, total):
    keyed = [
        [m[0][0] + m[1][1] + m[2][2], m[1][2] - m[2][1], m[2][0] - m[0][2], m[0][1] - m[1][0]],
        [m[1][2] - m[2][1], m[0][0] - m[1][1] - m[2][2], m[0][1] + m[1][0], m[2][0] + m[0][2]],
        [m[2][0] - m[0][2], m[0][1] + m[1][0], -m[0][0] + m[1][1] - m[2][2], m[1][2] + m[2][1]],
        [m[0][1] - m[1][0], m[2][0] + m[0][2], m[1][2] + m[2][1], -m[0][0] - m[1][1] + m[2][2]],
    ]
    top_one, top_two, low_one, low_two = keyed
    det_key = (
        pair_minor(top_one, top_two, 0, 1) * pair_minor(low_one, low_two, 2, 3)
        - pair_minor(top_one, top_two, 0, 2) * pair_minor(low_one, low_two, 1, 3)
        + pair_minor(top_one, top_two, 0, 3) * pair_minor(low_one, low_two, 1, 2)
        + pair_minor(top_one, top_two, 1, 2) * pair_minor(low_one, low_two, 0, 3)
        - pair_minor(top_one, top_two, 1, 3) * pair_minor(low_one, low_two, 0, 2)
        + pair_minor(top_one, top_two, 2, 3) * pair_minor(low_one, low_two, 0, 1)
    )
    det_three = (
        m[0][0] * (m[1][1] * m[2][2] - m[1][2] * m[2][1])
        - m[0][1] * (m[1][0] * m[2][2] - m[1][2] * m[2][0])
        + m[0][2] * (m[1][0] * m[2][1] - m[1][1] * m[2][0])
    )
    square_sum = m[0][0] * m[0][0]
    for first in range(3):
        for second in range(3):
            if first + second > 0:
                square_sum = square_sum + m[first][second] * m[first][second]
    second_coef = -2.0 * square_sum
    first_coef = -8.0 * det_three
    largest = 0.5 * total
    for newton_step in range(NEWTON):
        squared = largest * largest
        polynomial = squared * squared + second_coef * squared + first_coef * largest + det_key
        derivative = 4.0 * squared * largest + 2.0 * second_coef * largest + first_coef
        largest = largest - polynomial / derivative
    return total - 2.0 * largest


def split(value):
    high = value.astype(jnp.bfloat16)
    low = (value - high.astype(jnp.float32)).astype(jnp.bfloat16)
    return high, low


def kernel(n, reps, coords, count, both, own, part, cnt, pcnt, full, ft, gt, cov,
           fshift, fsum, gshift, gsum, col, dev, devt,
           zs, zr, fs, xs, pr, cs, cr, os, br, ar, ls, go):
    behind, ahead = both.at[0], both.at[1]
    b = lax.axis_index("blk")
    z = lax.axis_index("rep")
    par = lax.rem(b, 2)
    odd = lax.rem(b // 2, 2)
    bent = odd * par == 1
    bends = odd * (1 - par) == 1
    atoms = coords.shape[1]
    half = coords.shape[2] // 2
    quarter = half // 2
    natom = atoms * reps
    pitch = (atoms + 15) // 16 * 16
    again = full.shape[0]
    tail = ft.shape[3] - again
    g = z // 2
    o = 1 - g
    me = z
    fd = (reps - 1) * g
    of = reps - 1 - fd
    ot = reps - 1 - z
    wk = 1 + g
    inner = jnp.minimum(z, 1) * jnp.minimum(reps - 1 - z, 1)

    def at(step):
        return lax.rem(b + step + n, n)

    barrier = pltpu.get_barrier_semaphore()
    pl.semaphore_signal(barrier, inc=1, device_id=(at(1 - 2 * par), z), device_id_type=MESH)

    @pl.when(odd == 1)
    def _():
        pl.semaphore_signal(barrier, inc=1, device_id=(at(-2), z), device_id_type=MESH)

    @pl.when(par == 0)
    def _():
        pl.semaphore_signal(barrier, inc=1, device_id=(at(-3), z), device_id_type=MESH)

    @pl.when(odd + par == 1)
    def _():
        pl.semaphore_signal(barrier, inc=1, device_id=(at(1 - 2 * odd), z), device_id_type=MESH)

    @pl.when(inner == 1)
    def _():
        for where in (ot, fd):
            pl.semaphore_signal(barrier, inc=1, device_id=(b, where), device_id_type=MESH)

    pl.semaphore_wait(barrier, 3 + 2 * (1 - odd) * par)

    @pl.when((odd == 0) & (par == 1))
    def _():
        pl.semaphore_signal(go, inc=1, device_id=(at(1), z), device_id_type=MESH)

    def remote(src, dst, send, recv, where):
        return pltpu.make_async_remote_copy(src_ref=src, dst_ref=dst, send_sem=send, recv_sem=recv,
                                            device_id=where, device_id_type=MESH)

    def lanes(h):
        return pl.ds(pl.multiple_of(h * half, half), half)

    def source(s, h, k, mine):
        return coords.at[k, :, lanes(h)] if mine else own.at[s, h, k]

    def along(s, h, k, mine, where):
        return remote(source(s, h, k, mine), own.at[s, h, k], zs.at[1 - mine, h, k], zr.at[s, h, k],
                      (b, where))

    def first(s, k, mine):
        slot = 2 * par
        return remote(source(s, g, k, mine), part.at[slot, s, k], xs.at[1, s, k], pr.at[slot, s, k],
                      (at(1 + slot), z))

    def second(s, k, mine):
        return remote(source(s, g, k, mine), part.at[1, s, k], xs.at[0, s, k], pr.at[1, s, k],
                      (at(2), z))

    def bend(s, k):
        return remote(part.at[2, s, k], part.at[1, s, k], xs.at[3, s, k], pr.at[1, s, k],
                      (at(-1), z))

    def relay(s, k):
        slot = 2 - 2 * par
        return remote(part.at[1, s, k], part.at[slot, s, k], xs.at[2, s, k], pr.at[slot, s, k],
                      (at(1 - 2 * par), z))

    def feed(k):
        return remote(part.at[1, z, k], part.at[1, z, k], fs.at[k], pr.at[1, z, k], (b, wk))

    def count_first():
        slot = 2 * par
        return remote(cnt, pcnt.at[slot], cs.at[1], cr.at[slot], (at(1 + slot), z))

    def count_second():
        return remote(cnt, pcnt.at[1], cs.at[0], cr.at[1], (at(2), z))

    def count_bend():
        return remote(pcnt.at[2], pcnt.at[1], cs.at[3], cr.at[1], (at(-1), z))

    def count_relay():
        slot = 2 - 2 * par
        return remote(pcnt.at[1], pcnt.at[slot], cs.at[2], cr.at[slot], (at(1 - 2 * par), z))

    def zr_wait(s, h, k):
        remote(own.at[s, h, k], own.at[s, h, k], zs.at[0, h, k], zr.at[s, h, k],
               (b, lax.rem(z + 1, reps))).wait_recv()

    def pr_wait(d, s, k):
        remote(part.at[d, s, k], part.at[d, s, k], xs.at[0, s, k], pr.at[d, s, k],
               (b, lax.rem(z + 1, reps))).wait_recv()

    def cr_wait(d):
        remote(pcnt.at[d], pcnt.at[d], cs.at[0], cr.at[d], (b, lax.rem(z + 1, reps))).wait_recv()

    def local(h):
        return pltpu.make_async_copy(coords.at[:, :, lanes(h)], own.at[z, h], ls.at[h])

    def behind_copy(h, d, j):
        return remote(dev.at[h, d, pl.ds(j * quarter, quarter)], behind.at[d, :, lanes(g)],
                      os.at[h, d, 2 + j], br.at[d, g], (b, 2 * h + j))

    def ahead_copy(h, d, j):
        return remote(devt.at[h, d, pl.ds(j * quarter, quarter)], ahead.at[d, :, lanes(h)],
                      os.at[h, d, j], ar.at[d, h], (lax.rem(b - 1 - d + n, n), 2 * g + j))

    def ahead_wait(d, h):
        remote(devt.at[0, d, pl.ds(0, quarter)], ahead.at[d, :, pl.ds(h * half, half)],
               os.at[0, d, 0], ar.at[d, h], (at(1), z)).wait_recv()

    def behind_wait(d, side):
        remote(dev.at[0, d, pl.ds(0, quarter)], behind.at[d, :, lanes(side)],
               os.at[0, d, 2], br.at[d, side], (at(1), z)).wait_recv()

    def feeder():
        for k in range(3):
            along(me, o, k, True, wk).start()

            @pl.when(bent)
            def _(k=k):
                first(me, k, True).start()

        @pl.when(bends)
        def _():
            pl.semaphore_wait(go, 1)

        for k in range(3):
            @pl.when(jnp.logical_not(bent))
            def _(k=k):
                second(me, k, True).start()

        for k in range(3):
            along(me, g, k, True, wk).start()
        for k in range(3):
            turn(me, k)
        for k in range(3):
            pr_wait(1, me, k)
            feed(k).start()
        for k in range(3):
            along(me, o, k, True, wk).wait_send()
            along(me, g, k, True, wk).wait_send()
            feed(k).wait_send()

            @pl.when(bent)
            def _(k=k):
                first(me, k, True).wait_send()

            @pl.when(jnp.logical_not(bent))
            def _(k=k):
                second(me, k, True).wait_send()

            @pl.when(bends)
            def _(k=k):
                bend(me, k).wait_send()

        for d in range(ROUNDS):
            for side in range(2):
                behind_wait(d, side)
                ahead_wait(d, side)

    def across(s, k, mine):
        first(s, k, mine).start()

        @pl.when(jnp.logical_not(bent))
        def _():
            second(s, k, mine).start()

    def turn(s, k):
        @pl.when(bends)
        def _():
            pr_wait(2, s, k)
            bend(s, k).start()

    def pass_on(s, k):
        pr_wait(1, s, k)
        relay(s, k).start()

    def settle(s, bent_in):
        for k in range(3):
            pr_wait(0, s, k)

            if bent_in:
                @pl.when(jnp.logical_not(bends))
                def _(k=k):
                    pr_wait(2, s, k)
            else:
                pr_wait(2, s, k)

    def own_part(s, h, k, start):
        value = own[s, h, k]
        if start:
            shift = jnp.sum(value, axis=0, keepdims=True) / atoms
            fshift[h, k, 0:1, :] = shift
        else:
            shift = fshift[h, k, 0:1, :]
        value = value - shift
        total = jnp.sum(value, axis=0, keepdims=True)
        square = jnp.sum(value * value, axis=0, keepdims=True)
        fsum[h, k, 0:1, :] = fsum[h, k, 0:1, :] + total
        fsum[h, 3, 0:1, :] = fsum[h, 3, 0:1, :] + square
        high = value.astype(jnp.bfloat16).astype(jnp.float32)
        full[0:atoms, :] = high
        full[pitch:pitch + atoms, :] = value - high
        turned = full[...].T.astype(jnp.bfloat16)
        ft[h, s, k * half:(k + 1) * half, 0:again] = turned
        ft[h, s, k * half:(k + 1) * half, again:again + tail] = turned[:, 0:tail]

    def partner_part(s, start):
        for d in range(ROUNDS):
            for k in range(3):
                value = part[d, s, k]
                if start:
                    shift = jnp.sum(value, axis=0, keepdims=True) / atoms
                    gshift[d, k, 0:1, :] = shift
                else:
                    shift = gshift[d, k, 0:1, :]
                value = value - shift
                total = jnp.sum(value, axis=0, keepdims=True)
                square = jnp.sum(value * value, axis=0, keepdims=True)
                gsum[d, k, 0:1, :] = gsum[d, k, 0:1, :] + total
                gsum[d, 3, 0:1, :] = gsum[d, 3, 0:1, :] + square
                high, low = split(value)
                place = slice((3 * d + k) * half, (3 * d + k + 1) * half)
                gt[s, 0:atoms, place] = high
                gt[s, pitch:pitch + atoms, place] = high
                gt[s, again:again + atoms, place] = low

    product = functools.partial(jnp.dot, preferred_element_type=jnp.float32)

    def multiply(s, h, start=False):
        term = product(ft[h, s], gt[s])
        cov[h] = term if start else cov[h] + term

    def multiply_rows(s, h, k):
        rows = slice(k * half, (k + 1) * half)
        cov[h, rows, :] = cov[h, rows, :] + product(ft[h, s, rows, :], gt[s])

    def tile(h):
        square = fsum[h, 3, 0:1, :] / natom
        for k in range(3):
            mean = fsum[h, k, 0:1, :] / natom
            square = square - mean * mean
            col[k] = jnp.broadcast_to(mean, (half, half)).T
        col[3] = jnp.broadcast_to(square, (half, half)).T
        rows = half // 4

        def block(d, carry):
            mean = [gsum[d, k, 0:1, :] / natom for k in range(3)]
            other_square = gsum[d, 3, 0:1, :] / natom
            for k in range(3):
                other_square = other_square - mean[k] * mean[k]

            def chunk(i, inner_carry):
                r = pl.multiple_of(i * rows, rows)
                m = [[cov[h, pl.ds(k * half + r, rows), lanes(3 * d + l)] * (1.0 / natom)
                      - col[k, pl.ds(r, rows), :] * mean[l] for l in range(3)] for k in range(3)]
                total = col[3, pl.ds(r, rows), :] + other_square
                frame = h * half + r + lax.broadcasted_iota(jnp.int32, (rows, half), 0)
                other = g * half + lax.broadcasted_iota(jnp.int32, (rows, half), 1)
                mask = (frame < cnt[0:1, :]) & (other < pcnt[d, 0:1, :])
                dev[h, d, pl.ds(r, rows), :] = jnp.where(mask, deviation(m, total), 0.0)
                return inner_carry

            lax.fori_loop(0, half // rows, chunk, 0, unroll=True)
            for j in range(2):
                @pl.when(2 * h + j != z)
                def _(j=j):
                    behind_copy(h, d, j).start()

                @pl.when(2 * h + j == z)
                def _(j=j):
                    behind[d, :, lanes(g)] = dev[h, d, j * quarter:(j + 1) * quarter, :]

            devt[h, d] = dev[h, d].T
            for j in range(2):
                ahead_copy(h, d, j).start()
            return carry

        lax.fori_loop(0, ROUNDS, lambda i, c: block(lax.rem(i + 1, ROUNDS), c), 0)

    def worker():
        for k in range(3):
            along(me, o, k, True, ot).start()
            first(me, k, True).start()

        @pl.when(bends)
        def _():
            pl.semaphore_wait(go, 1)

        for k in range(3):
            @pl.when(jnp.logical_not(bent))
            def _(k=k):
                second(me, k, True).start()

        for h in range(2):
            local(h).start()
        cnt[...] = jnp.full(cnt.shape, count[0], jnp.int32)
        count_first().start()

        @pl.when(jnp.logical_not(bent))
        def _():
            count_second().start()

        full[...] = jnp.zeros_like(full)
        fsum[...] = jnp.zeros_like(fsum)
        gsum[...] = jnp.zeros_like(gsum)
        for h in range(2):
            local(h).wait()
        for k in range(3):
            own_part(me, g, k, True)
        for k in range(3):
            zr_wait(fd, o, k)
            along(fd, o, k, False, ot).start()
            zr_wait(ot, g, k)
            across(ot, k, False)
            turn(me, k)
            own_part(me, o, k, True)
            if k == 2:
                along(me, g, 0, True, ot).start()

        @pl.when(bends)
        def _():
            cr_wait(2)
            count_bend().start()

        for k in range(1, 3):
            along(me, g, k, True, ot).start()
        gt[...] = jnp.zeros_like(gt)
        for k in range(3):
            pass_on(me, k)
        cr_wait(1)
        count_relay().start()
        for k in range(3):
            own_part(ot, g, k, False)
        for k in range(3):
            zr_wait(fd, g, k)
            along(fd, g, k, False, ot).start()
            first(fd, k, False).start()
            zr_wait(of, g, k)
            across(of, k, False)
            turn(ot, k)
            if k == 0:
                settle(me, True)
                partner_part(me, True)
                multiply(me, g, True)
            if k == 1:
                multiply(me, o, True)
        for k in range(3):
            pass_on(ot, k)
        for k in range(3):
            own_part(fd, o, k, False)
            own_part(fd, g, k, False)
        settle(ot, True)
        partner_part(ot, False)
        multiply(ot, g)
        for k in range(3):
            turn(of, k)
            own_part(of, g, k, False)
        for k in range(3):
            zr_wait(ot, o, k)
            own_part(ot, o, k, False)
            multiply_rows(ot, o, k)
        for k in range(3):
            pass_on(fd, k)
        for k in range(3):
            pass_on(of, k)
        settle(fd, False)
        partner_part(fd, False)
        multiply(fd, g)
        multiply(fd, o)
        settle(of, True)
        partner_part(of, False)
        multiply(of, g)
        cr_wait(0)

        @pl.when(jnp.logical_not(bends))
        def _():
            cr_wait(2)

        tile(g)
        for k in range(3):
            zr_wait(of, o, k)
            own_part(of, o, k, False)
            multiply_rows(of, o, k)
        tile(o)
        finish()

    def finish():
        for k in range(3):
            for h in range(2):
                along(me, h, k, True, ot).wait_send()
                along(fd, h, k, False, ot).wait_send()
            for s in (me, ot, of):
                first(s, k, False).wait_send()
                relay(s, k).wait_send()

                @pl.when(jnp.logical_not(bent))
                def _(s=s, k=k):
                    second(s, k, False).wait_send()

                @pl.when(bends)
                def _(s=s, k=k):
                    bend(s, k).wait_send()

            relay(fd, k).wait_send()
            first(fd, k, False).wait_send()

        count_first().wait_send()
        count_relay().wait_send()

        @pl.when(jnp.logical_not(bent))
        def _():
            count_second().wait_send()

        @pl.when(bends)
        def _():
            count_bend().wait_send()

        for d in range(ROUNDS):
            for h in range(2):
                for j in range(2):
                    ahead_copy(h, d, j).wait_send()

                    @pl.when(2 * h + j != z)
                    def _(h=h, d=d, j=j):
                        behind_copy(h, d, j).wait_send()

                ahead_wait(d, h)
            behind_wait(d, o)

    @pl.when(inner == 0)
    def _():
        feeder()

    @pl.when(inner == 1)
    def _():
        worker()


def shards(n, reps, coords, frame_count):
    atoms, frames = coords.shape[1], coords.shape[2]
    half = frames // 2
    pitch = (atoms + 15) // 16 * 16
    again = (2 * pitch + 127) // 128 * 128
    depth = again + (pitch + 127) // 128 * 128
    f32, bf16 = jnp.float32, jnp.bfloat16
    dma = pltpu.SemaphoreType.DMA
    vmem = pl.BlockSpec(memory_space=pltpu.VMEM)
    result = jax.ShapeDtypeStruct((2, ROUNDS, frames // reps, frames), f32)
    made = pl.pallas_call(
        functools.partial(kernel, n, reps),
        out_shape=result,
        in_specs=[pl.BlockSpec(memory_space=pl.ANY), pl.BlockSpec(memory_space=pltpu.SMEM)],
        out_specs=vmem,
        scratch_shapes=[
            pltpu.VMEM((reps, 2, 3, atoms, half), f32),
            pltpu.VMEM((ROUNDS, reps, 3, atoms, half), f32),
            pltpu.VMEM((8, half), jnp.int32),
            pltpu.VMEM((ROUNDS, 8, half), jnp.int32),
            pltpu.VMEM((again, half), f32),
            pltpu.VMEM((2, reps, 3 * half, depth), bf16),
            pltpu.VMEM((reps, depth, ROUNDS * 3 * half), bf16),
            pltpu.VMEM((2, 3 * half, ROUNDS * 3 * half), f32),
            pltpu.VMEM((2, 3, 8, half), f32),
            pltpu.VMEM((2, 4, 8, half), f32),
            pltpu.VMEM((ROUNDS, 3, 8, half), f32),
            pltpu.VMEM((ROUNDS, 4, 8, half), f32),
            pltpu.VMEM((4, half, half), f32),
            pltpu.VMEM((2, ROUNDS, half, half), f32),
            pltpu.VMEM((2, ROUNDS, half, half), f32),
            dma((2, 2, 3)),
            dma((reps, 2, 3)),
            dma((3,)),
            dma((4, reps, 3)),
            dma((ROUNDS, reps, 3)),
            dma((4,)),
            dma((ROUNDS,)),
            dma((2, ROUNDS, 4)),
            dma((ROUNDS, 2)),
            dma((ROUNDS, 2)),
            dma((2,)),
            pltpu.SemaphoreType.REGULAR,
        ],
        compiler_params=pltpu.CompilerParams(collective_id=0, has_side_effects=True,
                                             vmem_limit_bytes=53 * 1024 * 1024),
    )(coords, frame_count.astype(jnp.int32))
    return made[0], made[1]


def solution(mesh):
    in_specs = (P(None, "rep", "blk"), P("blk"))
    out_specs = (P(None, ("blk", "rep"), None), P(None, ("blk", "rep"), None))
    body = functools.partial(shards, mesh.shape["blk"], mesh.shape["rep"])
    return jax.shard_map(body, mesh=mesh, in_specs=in_specs, out_specs=out_specs, check_vma=False)
```
